32 devices in a mesh: groups: 2 (over y), tiles: 4 (over z), folds: 2 (over x), sub: 2 (over core).
Axes of the slice: x: 2, y: 2, z: 4, core: 2. Of those that a mesh axis runs over, the one named last changes fastest.
Arguments:
- features: bfloat16 [2, 32, 16, 16, 1024], P('folds', ('groups', 'tiles', 'sub')), parts along dimension 1, may hold values from -6 to 6
- conv_first: bfloat16 [2, 3, 3, 3, 64, 32], P('folds'), may hold values from -0.15625 to 0.15625
- gain_first: float32 [2, 32], P('folds'), may hold values from 0.1 to 1.9
- shift_first: float32 [2, 32], P('folds'), may hold values from -3 to 3
- conv_second: bfloat16 [2, 3, 3, 3, 32, 32], P('folds'), may hold values from -0.21875 to 0.21875
- gain_second: float32 [2, 32], P('folds'), may hold values from 0.1 to 1.9
- shift_second: float32 [2, 32], P('folds'), may hold values from -3 to 3
- head_weight: bfloat16 [2, 32, 16], P('folds'), may hold values from -1 to 1
- head_bias: float32 [2, 16], P('folds'), may hold values from -4 to 4
- corners: int32 [32, 3], P(('groups', 'tiles', 'sub')), parts along dimension 0, may hold values from 0 to 48, as said below
- counts: int32 [8, 2], P('groups'), parts along dimension 0, may hold values from 0 to 2, as said below
Outputs:
- logits: float32 [128, 40, 640], P(('groups', 'tiles'), ('folds', 'sub')), parts along dimension 0
The draws below stay inside these ranges and needn't reach their ends.
There are 2 independent parts, one for each index of `groups`. The reference program is written for one: setup_inputs(seed, part) draws one part's arguments, and reference() takes and returns one part's arrays. A program takes and returns all parts, laid end to end along the dimension named above; an argument that names none is the same for every part. Nothing has to cross between parts.
Inputs may be any that keep to these rules, and one draw needn't show every extreme that they name: `corners`: for slot n = (t * 2 + s) * 2 + j, the z coordinate lies in [t * 16, (t + 1) * 16) and equals (3) * 16 in the last slab; x lies in [0, 24] and y in [0, 24]. counts[t, s] + counts[t xor (2), s] <= 2 for every t and s; some entry equals 2.
All inputs are finite; a program needn't handle non-finite values.
Results may differ from the reference program's by a relative error of at most 0.01.
Values may be sent and summed in bfloat16 or wider, within the bound.
A program may use at most 128 MiB of HBM per device.

```python
import jax
import jax.numpy as jnp
from jax import lax

CIN = 64
CH = 32
CLASSES = 16
WE = 16
CAP = 2
TZ = 16
VX = 40
VY = 40
FOLDS = 2
TILES = 4
HALVES = 2
WINDOWS = 16
VZ = 64


def draw_counts(key, part):
    subkeys = jax.random.split(jax.random.fold_in(key, 17), 5)
    half_tiles = TILES // 2
    grid_shape = (half_tiles, HALVES)
    totals = jax.random.randint(subkeys[0], grid_shape, CAP // 2, CAP + 1)
    lower_part = jax.random.randint(subkeys[1], grid_shape, 0, totals + 1)
    chosen_tile = jax.random.randint(subkeys[2], (), 0, half_tiles)
    chosen_half = jax.random.randint(subkeys[3], (), 0, HALVES)
    upper_side = jax.random.randint(subkeys[4], (), 0, 2)
    marked = (jnp.arange(half_tiles)[:, None] == chosen_tile) & (jnp.arange(HALVES)[None, :] == chosen_half)
    totals = jnp.where(marked, CAP, totals)
    lower_part = jnp.where(marked, CAP * (1 - upper_side), lower_part)
    return jnp.concatenate([lower_part, totals - lower_part], axis=0).astype(jnp.int32)


def draw_corners(key, part):
    subkeys = jax.random.split(jax.random.fold_in(key, 29), 3)
    total_windows = TILES * HALVES * CAP
    owner_tile = jnp.arange(total_windows) // (HALVES * CAP)
    offsets = jax.random.randint(subkeys[0], (total_windows,), 0, TZ)
    offsets = jnp.where(owner_tile == TILES - 1, 0, offsets)
    depth = owner_tile * TZ + offsets
    across = jax.random.randint(subkeys[1], (total_windows,), 0, VX - WE + 1)
    along = jax.random.randint(subkeys[2], (total_windows,), 0, VY - WE + 1)
    return jnp.stack([depth, across, along], axis=1).astype(jnp.int32)


def block_scale(rng, extent, shards, smallest, largest):
    factor_of, own = 1.0, jax.random.fold_in(rng, 6)
    for axis_at, blocks in shards:
        steps = jnp.exp(jax.random.uniform(jax.random.fold_in(own, axis_at), (blocks,), jnp.float32, smallest / len(shards), largest / len(shards)))
        factor_of = factor_of * jnp.repeat(steps, extent[axis_at] // blocks).reshape([-1 if axis == axis_at else 1 for axis in range(len(extent))])
    return factor_of


def gaussian(rng, extent, scale, bound, cuts=(), kind=jnp.bfloat16):
    array = jax.random.normal(rng, extent, jnp.float32) * scale
    if len(cuts) > 0:
        array = block_scale(rng, extent, cuts, -0.22, 0.18) * array
    return jnp.clip(array, min=-bound, max=bound).astype(kind)


def setup_inputs(seed: int = 0, part: int = 0) -> dict:
    splits = jax.random.split(jax.random.key(seed), 12)
    part_splits = jax.random.split(jax.random.fold_in(splits[11], part), 12)
    return {
        "features": gaussian(part_splits[0], (FOLDS, WINDOWS, WE, WE, WE * CIN), 1.0, 6.0, ((0, 2), (1, 8))),
        "conv_first": gaussian(splits[1], (FOLDS, 3, 3, 3, CIN, CH), (27 * CIN) ** -0.5, 0.15625, ((0, 2),)),
        "gain_first": jnp.clip(1.0 + 0.18 * jax.random.normal(splits[2], (FOLDS, CH), jnp.float32), 0.1, 1.9),
        "shift_first": gaussian(splits[3], (FOLDS, CH), 0.5, 3.0, ((0, 2),), jnp.float32),
        "conv_second": gaussian(splits[4], (FOLDS, 3, 3, 3, CH, CH), (27 * CH) ** -0.5, 0.21875, ((0, 2),)),
        "gain_second": jnp.clip(1.0 + 0.18 * jax.random.normal(splits[5], (FOLDS, CH), jnp.float32), 0.1, 1.9),
        "shift_second": gaussian(splits[6], (FOLDS, CH), 0.5, 3.0, ((0, 2),), jnp.float32),
        "head_weight": gaussian(splits[7], (FOLDS, CH, CLASSES), CH ** -0.5, 1.0, ((0, 2),)),
        "head_bias": gaussian(splits[8], (FOLDS, CLASSES), 1.0, 4.0, ((0, 2),), jnp.float32),
        "corners": draw_corners(jax.random.fold_in(jax.random.fold_in(splits[11], part), 71), part),
        "counts": draw_counts(jax.random.fold_in(jax.random.fold_in(splits[11], part), 71), part),
    }


epsilon = 1e-05
leak_slope = 0.01

def gauss_table():
    coords = jnp.arange(WE, dtype=jnp.float32)
    center = (WE - 1) / 2.0
    spread = WE / 4.0
    profile = jnp.exp(-(coords - center) ** 2 / (2.0 * spread * spread))
    return profile[:, None, None] * profile[None, :, None] * profile[None, None, :]

def convolve(inputs, kernel):
    return lax.conv_general_dilated(inputs, kernel, (1, 1, 1), 'SAME', dimension_numbers=('NDHWC', 'DHWIO', 'NDHWC'), preferred_element_type=jnp.float32)

def normalize(hidden, gain_vec, shift_vec):
    mean_value = lax.optimization_barrier(jnp.mean(hidden, axis=(1, 2, 3), keepdims=True))
    variance = lax.optimization_barrier(jnp.mean((hidden - mean_value) ** 2, axis=(1, 2, 3), keepdims=True))
    scaled = (hidden - mean_value) * lax.rsqrt(variance + epsilon) * gain_vec + shift_vec
    return jnp.where(scaled >= 0, scaled, leak_slope * scaled).astype(jnp.bfloat16)

def decode(windows, kernel_one, gain_one, shift_one, kernel_two, gain_two, shift_two, head_kernel, head_shift):
    count = windows.shape[0]
    inputs = windows.reshape(count, WE, WE, WE, CIN)
    normed_first = normalize(convolve(inputs, kernel_one), gain_one, shift_one)
    normed_second = normalize(convolve(normed_first, kernel_two), gain_two, shift_two)
    head = jnp.einsum('nzxyc,ck->nzxyk', normed_second.astype(jnp.float32), head_kernel.astype(jnp.float32))
    weighted = ((head + head_shift) * gauss_table()[None, :, :, :, None]).astype(jnp.bfloat16)
    return weighted.reshape(count, WE, WE, WE * CLASSES)

def reference(features, conv_first, gain_first, shift_first, conv_second, gain_second, shift_second, head_weight, head_bias, corners, counts):
    volume = jnp.zeros((VZ + WE, VX, VY * CLASSES), jnp.float32)
    live_mask = (jnp.arange(CAP, dtype=jnp.int32)[None, None, :] < counts[:, :, None]).reshape(-1).astype(jnp.float32)
    for fold_index in range(FOLDS):
        weighted = decode(features[fold_index], conv_first[fold_index], gain_first[fold_index], shift_first[fold_index], conv_second[fold_index], gain_second[fold_index], shift_second[fold_index], head_weight[fold_index], head_bias[fold_index])

        def add_one(slot_index, total):
            window_piece = weighted[slot_index].astype(jnp.float32) * live_mask[slot_index]
            corner_start = (corners[slot_index, 0].astype(jnp.int32), corners[slot_index, 1].astype(jnp.int32), (corners[slot_index, 2] * CLASSES).astype(jnp.int32))
            current = lax.dynamic_slice(total, corner_start, window_piece.shape)
            return lax.dynamic_update_slice(total, current + window_piece, corner_start)
        volume = lax.fori_loop(0, WINDOWS, add_one, volume)
    return volume[:VZ]
```

```python
import jax
import jax.numpy as jnp
from jax import lax
from jax.experimental import pallas as pl
from jax.experimental.pallas import tpu as pltpu
from jax.sharding import PartitionSpec as P

CH = 32
CLASSES = 16
WE = 16
TZ = 16
VX = 40
VY = 40
ROWS = WE * WE
WIDTH = WE * CH
WCLS = WE * CLASSES
LANES = VY * CLASSES

epsilon = 1e-05
leak_slope = 0.01

f32 = jnp.float32
bf16 = jnp.bfloat16
MESH = pl.DeviceIdType.MESH


def iota(shape, dim):
    return lax.broadcasted_iota(jnp.int32, shape, dim)


def one_hot(mask):
    return jnp.where(mask, 1.0, 0.0)


def spread_lanes(vec, width):
    n = vec.shape[1]
    pick = one_hot(iota((n, width), 0) == iota((n, width), 1) % n)
    return jnp.dot(vec, pick, precision=lax.Precision.HIGHEST, preferred_element_type=f32)


def build_first(taps_ref, band):
    cin = taps_ref.shape[1]
    pick = one_hot(iota((cin, 2 * cin), 0) == iota((cin, 2 * cin), 1) % cin).astype(bf16)
    twice = jnp.dot(taps_ref[...], pick, preferred_element_type=f32)
    low = iota((CH, 2 * cin), 1) < cin
    none = jnp.zeros((CH, 2 * cin), f32)
    for dz in range(3):
        groups = {}
        for dx in range(3):
            first = (dz * 3 + dx) * 3 * CH
            t0, t1, t2 = (twice[first + dy * CH : first + (dy + 1) * CH] for dy in range(3))
            t01 = jnp.where(low, t0, t1)
            t12 = jnp.where(low, t1, t2)
            t2n = jnp.where(low, t2, none)
            nt0 = jnp.where(low, none, t0)
            groups[dx] = jnp.concatenate(
                [jnp.concatenate([t01, t2n], axis=1), jnp.concatenate([nt0, t12], axis=1)], axis=0
            ).astype(bf16)
            groups[dx, "wrap"] = jnp.concatenate(
                [jnp.concatenate([t01, none], axis=1), jnp.concatenate([none, t12], axis=1)], axis=0
            ).astype(bf16)
        blank = jnp.zeros((2 * CH, 4 * cin), bf16)
        band[0, dz] = jnp.concatenate([groups[1], groups[0], groups[2], blank], axis=0)
        band[1, dz] = jnp.concatenate([groups[0], groups[1], blank, groups[2]], axis=0)
        band[2, dz] = jnp.concatenate(
            [groups[0, "wrap"], groups[1, "wrap"], blank, groups[2, "wrap"]], axis=0
        )


def build_second(taps_ref, band):
    pick = one_hot(iota((CH, 4 * CH), 0) == iota((CH, 4 * CH), 1) % CH).astype(bf16)
    spread = jnp.dot(taps_ref[...], pick, preferred_element_type=f32)
    group = iota((4 * CH, 4 * CH), 1) // CH
    none = jnp.zeros((CH, 4 * CH), f32)
    blank = jnp.zeros((4 * CH, 4 * CH), f32)
    for dz in range(3):
        slab = {}
        for dx in range(3):
            first = (dz * 3 + dx) * 3 * CH
            taps = spread[first : first + 3 * CH]
            slab[dx, 0] = jnp.concatenate([taps, none], axis=0)
            slab[dx, 1] = jnp.concatenate([none, taps], axis=0)

        def columns(*which):
            out = blank
            for g, key in enumerate(which):
                if key is not None:
                    out = jnp.where(group == g, slab[key], out)
            return out.astype(bf16)

        rows = slice(dz * 4 * CH, (dz + 1) * 4 * CH)
        band[0, rows, : 4 * CH] = columns((1, 0), (1, 1), (0, 0), (0, 1))
        band[0, rows, 4 * CH :] = columns((2, 0), (2, 1), None, None)
        band[1, rows, : 4 * CH] = columns((0, 0), (0, 1), (1, 0), (1, 1))
        band[1, rows, 4 * CH :] = columns(None, None, (2, 0), (2, 1))


def combine(even, odd):
    rows = even.shape[0]
    low = iota((rows, 128), 1) < 64
    across = iota((rows, 128), 0) % WE
    centre = jnp.where(low, even[:, :128], odd[:, :128])
    before = pltpu.roll(jnp.where(low, odd[:, :128], even[:, :128]), 64, 1)
    after = jnp.where(low, even[:, 128:], odd[:, 128:])
    return (
        centre
        + jnp.where(across == 0, 0.0, pltpu.roll(before, 1, 0))
        + jnp.where(across == WE - 1, 0.0, pltpu.roll(after, rows - 1, 0))
    )


def conv_first(padded, w, band, hidden):
    k = band.shape[3]
    step = k // 2

    def view(b):
        out = []
        for dz in range(3):
            rows = slice(dz * WE, dz * WE + ROWS)
            if b < 7:
                out.append(padded[w, rows, b * step : b * step + k])
            else:
                out.append(padded[w, rows, 7 * step :])
                out.append(padded[w, rows, :step])
        return jnp.concatenate(out, axis=1)

    def dot(b, kind):
        x = view(b)
        res = None
        for dz in range(3):
            part = lax.dot_general(
                x[:, dz * k : (dz + 1) * k], band[kind, dz], (((1,), (1,)), ((), ())), preferred_element_type=f32
            )
            res = part if res is None else res + part
        return res

    for q in range(4):
        even = dot(2 * q, 0)
        odd = dot(2 * q + 1, 2 if q == 3 else 1)
        hidden[:, q * 128 : (q + 1) * 128] = combine(even, odd)


def conv_second(evens, odds, w, band, hidden):
    for q in range(4):
        res = []
        for kind, src in enumerate((evens, odds)):
            x = jnp.concatenate(
                [src[w, dz * WE : dz * WE + ROWS, q * 128 : (q + 1) * 128] for dz in range(3)], axis=1
            )
            res.append(jnp.dot(x, band[kind], preferred_element_type=f32))
        hidden[:, q * 128 : (q + 1) * 128] = combine(*res)


def group_sum(row):
    by = row.shape[1] // 2
    while by >= CH:
        row = row + pltpu.roll(row, by, 1)
        by //= 2
    return row


def normalize(hidden, gain, shift):
    voxels = float(WE * WE * WE)
    mean_value = group_sum(jnp.sum(hidden, axis=0, keepdims=True)) / voxels
    centered = hidden - mean_value
    variance = group_sum(jnp.sum(centered * centered, axis=0, keepdims=True)) / voxels
    scaled = centered * (lax.rsqrt(variance + epsilon) * gain) + shift
    return jnp.where(scaled >= 0, scaled, leak_slope * scaled)


def store_normed(values, evens, odds, w):
    rows = slice(WE, WE + ROWS)
    lane = iota((ROWS, WIDTH), 1)
    evens[w, rows, :] = jnp.where(lane >= 15 * CH, 0.0, values).astype(bf16)
    turned = pltpu.roll(values, WIDTH - 2 * CH, 1)
    odds[w, rows, :] = jnp.where((lane >= 12 * CH) & (lane < 13 * CH), 0.0, turned).astype(bf16)


def head_of(values, corner, live, head_rows, bias):
    cz, cx, cy = corner
    row = iota((ROWS, ROWS), 0)
    source = ((row - cz) % WE) * WE + (row // WE - cx) % WE
    placed = one_hot(source == iota((ROWS, ROWS), 1)).astype(bf16)
    moved = jnp.dot(placed, values, preferred_element_type=f32).astype(bf16)
    y_in = iota((WIDTH, WCLS), 0) // CH + 2
    y_out = iota((WIDTH, WCLS), 1) // CLASSES
    head = jnp.where((y_out - cy - y_in) % WE == 0, head_rows, 0.0).astype(bf16)
    logits = jnp.dot(moved, head, preferred_element_type=f32) + bias
    centre = (WE - 1) / 2.0
    spread = 2.0 * (WE / 4.0) ** 2

    def bell(at):
        off = at.astype(f32) - centre
        return jnp.exp(-(off * off) / spread)

    rows = iota((ROWS, 1), 0)
    gauss_rows = bell((rows - cz) % WE) * bell((rows // WE - cx) % WE)
    gauss_rows = jnp.where(live, gauss_rows, 0.0)
    gauss_lanes = bell((iota((1, WCLS), 1) // CLASSES - cy) % WE)
    return (logits * (gauss_rows * gauss_lanes)).astype(bf16)


def head_table(head_weight):
    pick_rows = one_hot(iota((WIDTH, CH), 0) % CH == iota((WIDTH, CH), 1)).astype(bf16)
    pick_lanes = one_hot(iota((CLASSES, WCLS), 0) == iota((CLASSES, WCLS), 1) % CLASSES).astype(bf16)
    head_rows = lax.dot_general(
        pick_rows, head_weight, (((1,), (1,)), ((), ())), preferred_element_type=f32
    ).astype(bf16)
    return jnp.dot(head_rows, pick_lanes, preferred_element_type=f32)


def decode_send_kernel(
    features, taps_first, gain_first, shift_first, taps_second, gain_second, shift_second,
    head_weight, head_bias, corners, counts,
    own, sib, tail, tail_sib, meta,
    padded, evens, odds, band_first, band_second, hidden, ready, got,
    load_sems, x_send, x_recv, s_send, s_recv, z_send, z_recv, f_send, f_recv, m_send, m_recv,
):
    n = padded.shape[0]
    fold, sub, tile = (lax.axis_index(a) for a in ("folds", "sub", "tiles"))
    folds, subs, tiles = (lax.axis_size(a) for a in ("folds", "sub", "tiles"))
    span = VX // (folds * subs)
    edge = min(span, WE - span)
    both = 2 * span > WE
    loads = [
        pltpu.make_async_copy(features.at[w], padded.at[w, WE : WE + ROWS, :], load_sems.at[w])
        for w in range(n)
    ]
    for load in loads:
        load.start()

    barrier = pltpu.get_barrier_semaphore()

    def greet(where):
        pl.semaphore_signal(barrier, inc=1, device_id=where, device_id_type=MESH)

    other = {"sub": 1 - sub}
    greet(other)
    for d in range(1, folds):
        greet({"folds": lax.rem(fold + d, folds)})

    @pl.when(tile < tiles - 1)
    def _():
        greet({"tiles": tile + 1})

    @pl.when(tile > 0)
    def _():
        greet({"tiles": tile - 1})

    for w in range(n):
        for ref in (padded, evens, odds):
            ref[w, :WE, :] = jnp.zeros((WE, ref.shape[2]), bf16)
            ref[w, WE + ROWS :, :] = jnp.zeros((WE, ref.shape[2]), bf16)
    build_first(taps_first, band_first)
    build_second(taps_second, band_second)
    gains = [spread_lanes(g[...], WIDTH) for g in (gain_first, gain_second)]
    shifts = [spread_lanes(s[...], WIDTH) for s in (shift_first, shift_second)]
    head_rows = head_table(head_weight[...])
    bias = spread_lanes(head_bias[...], WCLS)
    live_count = counts[sub, tile]
    row_id = iota((8, 128), 0)
    corner_rows = jnp.zeros((8, 128), f32)
    for w in range(n):
        for c in range(3):
            at = corners[w, c].astype(f32)
            at = at - (tile * TZ).astype(f32) if c == 0 else at
            corner_rows = jnp.where(row_id == 3 * w + c, at, corner_rows)
    meta[0] = corner_rows

    pieces = [(jnp.where(sub == 0, 0, WE - edge), edge, True, False)]
    if both:
        pieces.append((edge, WE - 2 * edge, True, True))
    pieces.append((jnp.where(sub == 0, WE - edge, 0), edge, False, True))

    def start_of(f):
        return lax.rem(f * (subs * span) + span, WE)

    x_copies = {}
    for w in range(n):
        loads[w].wait()
        conv_first(padded, w, band_first, hidden.at[w])
        store_normed(normalize(hidden[w], gains[0], shifts[0]), evens, odds, w)
        conv_second(evens, odds, w, band_second, hidden.at[w])
        second = normalize(hidden[w], gains[1], shifts[1]).astype(bf16)
        out = head_of(
            second, (corners[w, 0], corners[w, 1], corners[w, 2]), w < live_count, head_rows, bias
        ).reshape(WE, WE, WCLS)
        ready[w, :WE] = out
        ready[w, WE:] = out
        if w == 0:
            peers = folds

            @pl.when((tile == 0) | (tile == tiles - 1))
            def _():
                pl.semaphore_wait(barrier, peers + 1)

            @pl.when((tile > 0) & (tile < tiles - 1))
            def _():
                pl.semaphore_wait(barrier, peers + 2)

            meta_sib = pltpu.make_async_remote_copy(
                src_ref=meta.at[0], dst_ref=meta.at[1], send_sem=m_send.at[0], recv_sem=m_recv.at[0],
                device_id=other, device_id_type=MESH,
            )
            meta_sib.start()
            meta_next = pltpu.make_async_remote_copy(
                src_ref=meta.at[0], dst_ref=meta.at[2], send_sem=m_send.at[1], recv_sem=m_recv.at[1],
                device_id={"tiles": lax.rem(tile + 1, tiles)}, device_id_type=MESH,
            )
            meta_on = pltpu.make_async_remote_copy(
                src_ref=meta.at[2], dst_ref=meta.at[3], send_sem=m_send.at[2], recv_sem=m_recv.at[2],
                device_id=other, device_id_type=MESH,
            )

            @pl.when(tile < tiles - 1)
            def _():
                meta_next.start()

        for c, (first, size, _, _) in enumerate(pieces):
            for d in range(1, folds):
                peer = lax.rem(fold + d, folds)
                copy = pltpu.make_async_remote_copy(
                    src_ref=ready.at[w, pl.ds(start_of(peer) + first, size)],
                    dst_ref=got.at[d - 1, w, pl.ds(first, size)],
                    send_sem=x_send.at[d - 1, w, c],
                    recv_sem=x_recv.at[d - 1, w, c],
                    device_id={"folds": peer},
                    device_id_type=MESH,
                )
                copy.start()
                x_copies[d, w, c] = copy

    s_copies, z_copies, f_copies = [], {}, []
    for w in range(n):
        for c, (first, size, theirs, _) in enumerate(pieces):
            rows = pl.ds(first, size)
            total = ready[w, pl.ds(start_of(fold) + first, size)].astype(f32)
            for d in range(1, folds):
                x_copies[d, w, c].wait_recv()
                total = total + got[d - 1, w, rows].astype(f32)
            own[w, rows] = total.astype(bf16)
            z_copies[w, c] = pltpu.make_async_remote_copy(
                src_ref=own.at[w, rows], dst_ref=tail.at[w, rows],
                send_sem=z_send.at[w, c], recv_sem=z_recv.at[w, c],
                device_id={"tiles": lax.rem(tile + 1, tiles)}, device_id_type=MESH,
            )

            @pl.when(tile < tiles - 1)
            def _():
                z_copies[w, c].start()

            if theirs:
                copy = pltpu.make_async_remote_copy(
                    src_ref=own.at[w, rows], dst_ref=sib.at[w, rows],
                    send_sem=s_send.at[w, c], recv_sem=s_recv.at[w, c],
                    device_id=other, device_id_type=MESH,
                )
                copy.start()
                s_copies.append(copy)

    for w in range(n):
        for c, (first, size, theirs, _) in enumerate(pieces):
            if theirs:
                f_copies.append(
                    pltpu.make_async_remote_copy(
                        src_ref=tail.at[w, pl.ds(first, size)], dst_ref=tail_sib.at[w, pl.ds(first, size)],
                        send_sem=f_send.at[w, c], recv_sem=f_recv.at[w, c],
                        device_id=other, device_id_type=MESH,
                    )
                )

    @pl.when(tile > 0)
    def _():
        meta_next.wait_recv()
        meta_on.start()
        k = 0
        for w in range(n):
            for c, (_, _, theirs, _) in enumerate(pieces):
                z_copies[w, c].wait_recv()
                if theirs:
                    f_copies[k].start()
                    k += 1
        meta_on.wait()
        for copy in f_copies:
            copy.wait()

    meta_sib.wait()
    for copy in s_copies:
        copy.wait()
    for copy in x_copies.values():
        copy.wait_send()

    @pl.when(tile < tiles - 1)
    def _():
        meta_next.wait_send()
        for copy in z_copies.values():
            copy.wait_send()


def decode_send(features, taps_first, gf, sf, taps_second, gs, ss, hw, hb, corners, counts):
    n = features.shape[0]
    in_width = features.shape[-1]
    cin = in_width // WE
    folds, subs = lax.axis_size("folds"), lax.axis_size("sub")
    vmem = pl.BlockSpec(memory_space=pltpu.VMEM)
    smem = pl.BlockSpec(memory_space=pltpu.SMEM)
    dma = pltpu.SemaphoreType.DMA
    block = pltpu.VMEM((n, WE, WE, WCLS), bf16)
    return pl.pallas_call(
        decode_send_kernel,
        out_shape=[block] * 4 + [pltpu.VMEM((4, 8, 128), f32)],
        in_specs=[pl.BlockSpec(memory_space=pltpu.HBM)] + [vmem] * 8 + [smem] * 2,
        out_specs=[vmem] * 5,
        scratch_shapes=[
            pltpu.VMEM((n, ROWS + 2 * WE, in_width), bf16),
            pltpu.VMEM((n, ROWS + 2 * WE, WIDTH), bf16),
            pltpu.VMEM((n, ROWS + 2 * WE, WIDTH), bf16),
            pltpu.VMEM((3, 3, 8 * CH, 4 * cin), bf16),
            pltpu.VMEM((2, 12 * CH, 8 * CH), bf16),
            pltpu.VMEM((n, ROWS, WIDTH), f32),
            pltpu.VMEM((n, 2 * WE, WE, WCLS), bf16),
            pltpu.VMEM((folds - 1, n, WE, WE, WCLS), bf16),
            dma((n,)),
            dma((folds - 1, n, 3)),
            dma((folds - 1, n, 3)),
            dma((n, 3)),
            dma((n, 3)),
            dma((n, 3)),
            dma((n, 3)),
            dma((n, 3)),
            dma((n, 3)),
            dma((3,)),
            dma((3,)),
        ],
        compiler_params=pltpu.CompilerParams(
            collective_id=0, has_side_effects=True, vmem_limit_bytes=56 * 1024 * 1024
        ),
    )(
        features.reshape(n, ROWS, in_width),
        taps_first.swapaxes(-1, -2).reshape(27 * CH, cin),
        gf,
        sf,
        taps_second.reshape(27 * CH, CH),
        gs,
        ss,
        hw.T,
        hb,
        corners,
        counts.T,
    )


def place_kernel(own, sib, tail, tail_sib, meta, out):
    n = own.shape[0]
    fold, sub, tile = (lax.axis_index(a) for a in ("folds", "sub", "tiles"))
    subs = lax.axis_size("sub")
    span = out.shape[0]
    lane_y = iota((1, LANES), 1) // CLASSES
    depth = iota((TZ, 1), 0)
    repeats = -(-LANES // 128)
    x0 = (fold * subs + sub) * span
    base = (1 - sub) * (WE - span)
    sources = []
    for k, ref in enumerate((own, sib, tail, tail_sib)):
        for w in range(n):
            cz, cx, cy = (meta[k, 3 * w + c : 3 * w + c + 1, :].astype(jnp.int32) for c in range(3))
            wide = [jnp.concatenate([v] * repeats, axis=1)[:, :LANES] for v in (cz, cx, cy)]
            inside = (lane_y >= wide[2]) & (lane_y < wide[2] + WE)
            deep = (depth >= wide[0]) if k < 2 else ((depth < wide[0]) & (tile > 0))
            sources.append((ref, w, inside & deep, wide[1]))
    for i in range(span):
        total = jnp.zeros((TZ, LANES), f32)
        for ref, w, mask, cx in sources:
            part = ref[w, base + i].astype(f32)
            wide = jnp.concatenate([part] * -(-LANES // WCLS), axis=1)[:, :LANES]
            x = x0 + i
            total = total + jnp.where(mask & (cx <= x) & (x < cx + WE), wide, 0.0)
        out[i] = total


def place(own, sib, tail, tail_sib, meta):
    span = VX // (lax.axis_size("folds") * lax.axis_size("sub"))
    vmem = pl.BlockSpec(memory_space=pltpu.VMEM)
    return pl.pallas_call(
        place_kernel,
        out_shape=jax.ShapeDtypeStruct((span, TZ, LANES), f32),
        in_specs=[vmem] * 5,
        out_specs=vmem,
        compiler_params=pltpu.CompilerParams(vmem_limit_bytes=12 * 1024 * 1024),
    )(own, sib, tail, tail_sib, meta)


def on_device(features, conv_one, gain_one, shift_one, conv_two, gain_two, shift_two, head_weight, head_bias, corners, counts):
    blocks = decode_send(
        features[0], conv_one[0], gain_one, shift_one, conv_two[0], gain_two, shift_two,
        head_weight[0], head_bias, corners, counts,
    )
    return place(*blocks).transpose(1, 0, 2)


def solution(mesh):
    windows = ("groups", "tiles", "sub")
    placed = (
        P("folds", windows, None, None, None),
        P("folds", None, None, None, None, None),
        P("folds", None),
        P("folds", None),
        P("folds", None, None, None, None, None),
        P("folds", None),
        P("folds", None),
        P("folds", None, None),
        P("folds", None),
        P(windows, None),
        P("groups", None),
    )
    return jax.shard_map(
        on_device,
        mesh=mesh,
        in_specs=placed,
        out_specs=P(("groups", "tiles"), ("folds", "sub"), None),
        check_vma=False,
    )
```

```python
import jax
import jax.numpy as jnp
from jax import lax
from jax.experimental import pallas as pl
from jax.experimental.pallas import tpu as pltpu
from jax.sharding import PartitionSpec as P

CH = 32
CLASSES = 16
WE = 16
TZ = 16
VX = 40
VY = 40
ROWS = WE * WE
WIDTH = WE * CH
WCLS = WE * CLASSES
LANES = VY * CLASSES

epsilon = 1e-05
leak_slope = 0.01

f32 = jnp.float32
bf16 = jnp.bfloat16
MESH = pl.DeviceIdType.MESH


def iota(shape, dim):
    return lax.broadcasted_iota(jnp.int32, shape, dim)


def one_hot(mask):
    return jnp.where(mask, 1.0, 0.0)


def spread_lanes(vec, width):
    n = vec.shape[1]
    pick = one_hot(iota((n, width), 0) == iota((n, width), 1) % n)
    return jnp.dot(vec, pick, precision=lax.Precision.HIGHEST, preferred_element_type=f32)


def build_first(taps_ref, band):
    cin = taps_ref.shape[1]
    pick = one_hot(iota((cin, 2 * cin), 0) == iota((cin, 2 * cin), 1) % cin).astype(bf16)
    twice = jnp.dot(taps_ref[...], pick, preferred_element_type=f32)
    low = iota((CH, 2 * cin), 1) < cin
    none = jnp.zeros((CH, 2 * cin), f32)
    blank = jnp.zeros((2 * CH, 4 * cin), bf16)
    for dz in range(3):
        groups, wrap = [], []
        for dx in range(3):
            first = (dz * 3 + dx) * 3 * CH
            t0, t1, t2 = (twice[first + dy * CH : first + (dy + 1) * CH] for dy in range(3))
            t01 = jnp.where(low, t0, t1)
            t12 = jnp.where(low, t1, t2)
            lower = jnp.concatenate([t01, jnp.where(low, t2, none)], axis=1)
            upper = jnp.concatenate([jnp.where(low, none, t0), t12], axis=1)
            groups.append(jnp.concatenate([lower, upper], axis=0).astype(bf16))
            lower = jnp.concatenate([t01, none], axis=1)
            upper = jnp.concatenate([none, t12], axis=1)
            wrap.append(jnp.concatenate([lower, upper], axis=0).astype(bf16))
        lanes = slice(dz * 4 * cin, (dz + 1) * 4 * cin)
        band[0, :, lanes] = jnp.concatenate([groups[1], groups[0], groups[2], blank], axis=0)
        band[1, :, lanes] = jnp.concatenate([groups[0], groups[1], blank, groups[2]], axis=0)
        band[2, :, lanes] = jnp.concatenate([wrap[0], wrap[1], blank, wrap[2]], axis=0)


def build_second(taps_ref, band):
    pick = one_hot(iota((CH, 4 * CH), 0) == iota((CH, 4 * CH), 1) % CH).astype(bf16)
    spread = jnp.dot(taps_ref[...], pick, preferred_element_type=f32)
    group = iota((4 * CH, 4 * CH), 1) // CH
    none = jnp.zeros((CH, 4 * CH), f32)
    blank = jnp.zeros((4 * CH, 4 * CH), f32)
    for dz in range(3):
        slab = {}
        for dx in range(3):
            first = (dz * 3 + dx) * 3 * CH
            taps = spread[first : first + 3 * CH]
            slab[dx, 0] = jnp.concatenate([taps, none], axis=0)
            slab[dx, 1] = jnp.concatenate([none, taps], axis=0)

        def columns(*which):
            out = blank
            for g, key in enumerate(which):
                if key is not None:
                    out = jnp.where(group == g, slab[key], out)
            return out.astype(bf16)

        rows = slice(dz * 4 * CH, (dz + 1) * 4 * CH)
        band[0, rows, : 4 * CH] = columns((1, 0), (1, 1), (0, 0), (0, 1))
        band[0, rows, 4 * CH :] = columns((2, 0), (2, 1), None, None)
        band[1, rows, : 4 * CH] = columns((0, 0), (0, 1), (1, 0), (1, 1))
        band[1, rows, 4 * CH :] = columns(None, None, (2, 0), (2, 1))


def combine(even, odd):
    rows = even.shape[0]
    low = iota((rows, 128), 1) < 64
    across = iota((rows, 128), 0) % WE
    centre = jnp.where(low, even[:, :128], odd[:, :128])
    before = pltpu.roll(jnp.where(low, odd[:, :128], even[:, :128]), 64, 1)
    after = jnp.where(low, even[:, 128:], odd[:, 128:])
    return (
        centre
        + jnp.where(across == 0, 0.0, pltpu.roll(before, 1, 0))
        + jnp.where(across == WE - 1, 0.0, pltpu.roll(after, rows - 1, 0))
    )


def view_first(padded, w, b, step):
    out = []
    for dz in range(3):
        rows = slice(dz * WE, dz * WE + ROWS)
        if b < 7:
            out.append(padded[w, rows, b * step : (b + 2) * step])
        else:
            out.append(padded[w, rows, 7 * step :])
            out.append(padded[w, rows, :step])
    return jnp.concatenate(out, axis=1)


def conv_first(padded, w, band, hidden, quarters):
    step = padded.shape[2] // 8
    for q in quarters:
        res = [
            lax.dot_general(
                view_first(padded, w, 2 * q + odd, step),
                band[kind],
                (((1,), (1,)), ((), ())),
                preferred_element_type=f32,
            )
            for odd, kind in ((0, 0), (1, 2 if q == 3 else 1))
        ]
        hidden[:, q * 128 : (q + 1) * 128] = combine(*res)


def conv_second(evens, odds, w, band, hidden, quarters):
    for q in quarters:
        res = [
            jnp.dot(
                jnp.concatenate(
                    [src[w, dz * WE : dz * WE + ROWS, q * 128 : (q + 1) * 128] for dz in range(3)], axis=1
                ),
                band[kind],
                preferred_element_type=f32,
            )
            for kind, src in enumerate((evens, odds))
        ]
        hidden[:, q * 128 : (q + 1) * 128] = combine(*res)


def over_voxels(row):
    row = row + pltpu.roll(row, 64, 1)
    return row + pltpu.roll(row, 32, 1)


def partial_sum(block):
    return jnp.sum(block.reshape(ROWS // 8, 8, 128), axis=0)


def statistics(hidden, gain):
    voxels = float(WE * WE * WE)
    about = over_voxels(hidden[:1, :128]) / 4.0
    first, square = None, None
    for q in range(4):
        off = hidden[:, q * 128 : (q + 1) * 128] - about
        parts = partial_sum(off), partial_sum(off * off)
        first = parts[0] if first is None else first + parts[0]
        square = parts[1] if square is None else square + parts[1]
    first = over_voxels(jnp.sum(first, axis=0, keepdims=True)) / voxels
    square = over_voxels(jnp.sum(square, axis=0, keepdims=True)) / voxels
    variance = jnp.maximum(square - first * first, 0.0)
    return about + first, lax.rsqrt(variance + epsilon) * gain


def normalize(hidden, stats, shift):
    mean_value, factor = stats
    out = []
    for q in range(4):
        scaled = (hidden[:, q * 128 : (q + 1) * 128] - mean_value) * factor + shift
        out.append(jnp.maximum(scaled, leak_slope * scaled))
    return out


def store_normed(values, evens, odds, w):
    rows = slice(WE, WE + ROWS)
    lane = iota((ROWS, 128), 1)
    low = lane < 64
    for q in range(4):
        even = values[q] if q < 3 else jnp.where(lane >= 96, 0.0, values[q])
        evens[w, rows, q * 128 : (q + 1) * 128] = even.astype(bf16)
        odd = pltpu.roll(jnp.where(low, values[(q + 1) % 4], values[q]), 64, 1)
        odd = odd if q < 3 else jnp.where(lane < 32, 0.0, odd)
        odds[w, rows, q * 128 : (q + 1) * 128] = odd.astype(bf16)


def bell(at):
    off = at.astype(f32) - (WE - 1) / 2.0
    return -(off * off) / (2.0 * (WE / 4.0) ** 2)


def prepare_head(corner, live, head_weight, placed, head, gauss):
    cz, cx, cy = corner
    row = iota((ROWS, 128), 0)
    lane = iota((ROWS, 128), 1)
    source = ((row - cz) & (WE - 1)) * WE + ((lax.shift_right_logical(row, 4) - cx) & (WE - 1))
    for half in range(2):
        lanes = slice(half * 128, (half + 1) * 128)
        placed[:, lanes] = one_hot(source == lane + half * 128).astype(bf16)
        z, x = lax.shift_right_logical(row, 4), row & (WE - 1)
        y = (lax.shift_right_logical(lane, 4) + half * 8 - cy) & (WE - 1)
        gauss[:, lanes] = jnp.where(live, jnp.exp(bell(z) + bell(x) + bell(y)), 0.0)
    at = lax.shift_right_logical(iota((CH, WCLS), 1), 4) - cy
    for u in range(WE):
        head[u * CH : (u + 1) * CH, :] = jnp.where(((at - u - 2) & (WE - 1)) == 0, head_weight, 0.0).astype(bf16)


def apply_head(values, placed, head, gauss, bias):
    second = jnp.concatenate([v.astype(bf16) for v in values], axis=1)
    logits = jnp.dot(second, head[...], preferred_element_type=f32) + bias
    weighted = (logits * gauss[...]).astype(bf16)
    return jnp.dot(placed[...], weighted, preferred_element_type=f32).astype(bf16)


def decode_send_kernel(
    features, taps_first, gain_first, shift_first, taps_second, gain_second, shift_second,
    head_weight, head_bias, corners_in, counts_in,
    own, sib, tail, tail_sib, direct, meta,
    padded, evens, odds, band_first, band_second, hidden, ready, got, placed, head, gauss,
    taps_one, taps_two, gains, weights, biases, corners, counts,
    load_sems, in_sems, x_send, x_recv, s_send, s_recv, z_send, z_recv, f_send, f_recv, d_send, d_recv, m_send, m_recv,
):
    n = padded.shape[0]
    fold, sub, tile = (lax.axis_index(a) for a in ("folds", "sub", "tiles"))
    folds, subs, tiles = (lax.axis_size(a) for a in ("folds", "sub", "tiles"))
    span = VX // (folds * subs)
    edge = min(span, WE - span)
    loads = [
        pltpu.make_async_copy(features.at[w], padded.at[w, WE : WE + ROWS, :], load_sems.at[w])
        for w in range(n)
    ]
    small = [
        pltpu.make_async_copy(src, dst, in_sems.at[k])
        for k, (src, dst) in enumerate(
            (
                (corners_in, corners),
                (counts_in, counts),
                (head_weight, weights),
                (taps_first, taps_one),
                (taps_second, taps_two),
                (head_bias, biases),
                (gain_first, gains.at[0]),
                (shift_first, gains.at[1]),
                (gain_second, gains.at[2]),
                (shift_second, gains.at[3]),
            )
        )
    ]
    for copy in small[:5]:
        copy.start()
    loads[0].start()
    for copy in small[5:]:
        copy.start()
    for load in loads[1:]:
        load.start()

    barrier = pltpu.get_barrier_semaphore()
    other = 1 - sub
    later, earlier = lax.rem(tile + 1, tiles), lax.rem(tile + tiles - 1, tiles)

    def greet(**where):
        pl.semaphore_signal(barrier, inc=1, device_id=where, device_id_type=MESH)

    def greet_tile(at):
        greet(tiles=at)
        greet(tiles=at, sub=other)
        for d in range(1, folds):
            greet(tiles=at, folds=lax.rem(fold + d, folds))

    greet(sub=other)
    for d in range(1, folds):
        greet(folds=lax.rem(fold + d, folds))

    @pl.when(tile < tiles - 1)
    def _():
        greet_tile(tile + 1)

    @pl.when(tile > 0)
    def _():
        greet_tile(tile - 1)

    for w in range(n):
        for ref in (padded, evens, odds):
            ref[w, :WE, :] = jnp.zeros((WE, ref.shape[2]), bf16)
            ref[w, WE + ROWS :, :] = jnp.zeros((WE, ref.shape[2]), bf16)
    for copy in small[:3]:
        copy.wait()
    pick = one_hot(iota((CLASSES, WCLS), 0) == iota((CLASSES, WCLS), 1) % CLASSES)
    head_rows = lax.dot_general(
        weights[...], pick.astype(bf16), (((0,), (0,)), ((), ())), preferred_element_type=f32
    )
    live_count = counts[sub, tile]
    for w in range(n):
        corner = corners[w, 0], corners[w, 1], corners[w, 2]
        prepare_head(corner, w < live_count, head_rows, placed.at[w], head.at[w], gauss.at[w])
    row_id = iota((8, 128), 0)
    corner_rows = jnp.zeros((8, 128), f32)
    for w in range(n):
        for c in range(3):
            at = corners[w, c].astype(f32)
            at = at - (tile * TZ).astype(f32) if c == 0 else at
            corner_rows = jnp.where(row_id == 3 * w + c, at, corner_rows)
    meta[0] = corner_rows
    for copy in small[3:]:
        copy.wait()
    build_first(taps_one, band_first)
    build_second(taps_two, band_second)
    gain_one, shift_one, gain_two, shift_two = (spread_lanes(gains[k], 128) for k in range(4))
    bias = spread_lanes(biases[...], WCLS)

    theirs = (jnp.where(sub == 0, 0, WE - edge), edge)
    shared = (edge, WE - 2 * edge)
    mine = (jnp.where(sub == 0, WE - edge, 0), edge)
    parts = {"theirs": theirs, "mine": mine}
    if 2 * span > WE:
        parts["shared"] = shared
    order = [p for p in ("shared", "theirs", "mine") if p in parts]
    index = {"theirs": 0, "shared": 1, "mine": 2}

    def start_of(f):
        return lax.rem(f * (subs * span) + span, WE)

    def remote(src, dst, sems, at, **where):
        return pltpu.make_async_remote_copy(
            src_ref=src, dst_ref=dst, send_sem=sems[0].at[at], recv_sem=sems[1].at[at],
            device_id=where, device_id_type=MESH,
        )

    x_copies, s_copies, z_copies, d_copies, f_copies = {}, {}, {}, [], {}
    metas = [
        remote(meta.at[0], meta.at[1], (m_send, m_recv), 0, sub=other),
        remote(meta.at[0], meta.at[2], (m_send, m_recv), 1, tiles=later),
        remote(meta.at[0], meta.at[3], (m_send, m_recv), 2, tiles=later, sub=other),
    ]

    def norm_one(w):
        stats[w, 1] = statistics(hidden.at[w], gain_one)

    def store_one(w):
        store_normed(normalize(hidden.at[w], stats[w, 1], shift_one), evens, odds, w)

    def norm_two(w):
        stats[w, 2] = statistics(hidden.at[w], gain_two)

    def values_two(w):
        values[w] = normalize(hidden.at[w], stats[w, 2], shift_two)

    def finish(w):
        out = apply_head(values[w], placed.at[w], head.at[w], gauss.at[w], bias).reshape(WE, WE, WCLS)
        ready[w, :WE] = out
        ready[w, WE:] = out

    stats, values = {}, {}

    def send(w):
        if w == 0:
            near = folds

            @pl.when((tile == 0) | (tile == tiles - 1))
            def _():
                pl.semaphore_wait(barrier, near + folds + 1)

            @pl.when((tile > 0) & (tile < tiles - 1))
            def _():
                pl.semaphore_wait(barrier, near + 2 * (folds + 1))

        for name in order:
            first, size = parts[name]
            for d in range(1, folds):
                peer = lax.rem(fold + d, folds)
                copy = remote(
                    ready.at[w, pl.ds(start_of(peer) + first, size)],
                    got.at[d - 1, w, pl.ds(first, size)],
                    (x_send, x_recv), (d - 1, w, index[name]), folds=peer,
                )
                copy.start()
                x_copies[d, w, name] = copy
        if w == 0:
            metas[0].start()

            @pl.when(tile < tiles - 1)
            def _():
                for copy in metas[1:]:
                    copy.start()

        if w == n - 1:
            first, size = mine
            for d in range(folds):
                peer = lax.rem(fold + d, folds)
                where = {"tiles": later} if d == 0 else {"tiles": later, "folds": peer}
                d_copies.append(
                    remote(
                        ready.at[w, pl.ds(start_of(peer) + first, size)],
                        direct.at[d], (d_send, d_recv), d, **where
                    )
                )

            @pl.when(tile < tiles - 1)
            def _():
                for copy in d_copies:
                    copy.start()

    def first(w, *quarters):
        conv_first(padded, w, band_first, hidden.at[w], quarters)

    def second(w, *quarters):
        conv_second(evens, odds, w, band_second, hidden.at[w], quarters)

    loads[0].wait()
    loads[1].wait()
    first(0, 0, 1, 2, 3)
    norm_one(0)
    first(1, 0, 1)
    store_one(0)
    second(0, 0, 1, 2, 3)
    first(1, 2, 3)
    norm_two(0)
    norm_one(1)
    values_two(0)
    finish(0)
    send(0)
    store_one(1)
    second(1, 0, 1, 2, 3)
    norm_two(1)
    values_two(1)
    finish(1)
    send(1)

    def gather(w, name):
        first, size = parts[name]
        rows = pl.ds(first, size)
        total = ready[w, pl.ds(start_of(fold) + first, size)].astype(f32)
        for d in range(1, folds):
            x_copies[d, w, name].wait_recv()
            total = total + got[d - 1, w, rows].astype(f32)
        own[w, rows] = total.astype(bf16)
        at = w, index[name]
        if name == "theirs":
            z_copies[at] = remote(
                own.at[w, rows], tail_sib.at[w, rows], (z_send, z_recv), at, tiles=later, sub=other
            )
        elif name == "shared" or w < n - 1:
            z_copies[at] = remote(own.at[w, rows], tail.at[w, rows], (z_send, z_recv), at, tiles=later)
        if at in z_copies:

            @pl.when(tile < tiles - 1)
            def _():
                z_copies[at].start()

        if name != "mine":
            s_copies[at] = remote(own.at[w, rows], sib.at[w, rows], (s_send, s_recv), at, sub=other)
            s_copies[at].start()

    def forward(w):
        if "shared" in parts:
            rows = pl.ds(*parts["shared"])
            f_copies[w] = remote(tail.at[w, rows], tail_sib.at[w, rows], (f_send, f_recv), w, sub=other)

            @pl.when(tile > 0)
            def _():
                z_copies[w, index["shared"]].wait_recv()
                f_copies[w].start()

    for w in range(n - 1):
        for name in order:
            gather(w, name)
    for name in order[:-1]:
        gather(n - 1, name)
    for w in range(n - 1):
        forward(w)
    gather(n - 1, order[-1])
    forward(n - 1)

    @pl.when(tile > 0)
    def _():
        for copy in metas[1:] + d_copies:
            copy.wait_recv()
        for at, copy in z_copies.items():
            if at[1] != index["shared"]:
                copy.wait_recv()
        for copy in f_copies.values():
            copy.wait()

    metas[0].wait()
    for copy in s_copies.values():
        copy.wait()
    for copy in x_copies.values():
        copy.wait_send()

    @pl.when(tile < tiles - 1)
    def _():
        for copy in metas[1:] + d_copies + list(z_copies.values()):
            copy.wait_send()


def decode_send(features, taps_first, gf, sf, taps_second, gs, ss, hw, hb, corners, counts):
    n = features.shape[0]
    in_width = features.shape[-1]
    cin = in_width // WE
    folds, subs, tiles = (lax.axis_size(a) for a in ("folds", "sub", "tiles"))
    span = VX // (folds * subs)
    edge = min(span, WE - span)
    hbm = pl.BlockSpec(memory_space=pltpu.HBM)
    vmem = pl.BlockSpec(memory_space=pltpu.VMEM)
    dma = pltpu.SemaphoreType.DMA
    block = pltpu.VMEM((n, WE, WE, WCLS), bf16)
    return pl.pallas_call(
        decode_send_kernel,
        out_shape=[block] * 4 + [pltpu.VMEM((folds, edge, WE, WCLS), bf16), pltpu.VMEM((4, 8, 128), f32)],
        in_specs=[hbm] * 11,
        out_specs=[vmem] * 6,
        scratch_shapes=[
            pltpu.VMEM((n, ROWS + 2 * WE, in_width), bf16),
            pltpu.VMEM((n, ROWS + 2 * WE, WIDTH), bf16),
            pltpu.VMEM((n, ROWS + 2 * WE, WIDTH), bf16),
            pltpu.VMEM((3, 8 * CH, 12 * cin), bf16),
            pltpu.VMEM((2, 12 * CH, 8 * CH), bf16),
            pltpu.VMEM((n, ROWS, WIDTH), f32),
            pltpu.VMEM((n, 2 * WE, WE, WCLS), bf16),
            pltpu.VMEM((folds - 1, n, WE, WE, WCLS), bf16),
            pltpu.VMEM((n, ROWS, ROWS), bf16),
            pltpu.VMEM((n, WIDTH, WCLS), bf16),
            pltpu.VMEM((n, ROWS, WCLS), f32),
            pltpu.VMEM((27 * CH, cin), bf16),
            pltpu.VMEM((27 * CH, CH), bf16),
            pltpu.VMEM((4, 1, CH), f32),
            pltpu.VMEM((CLASSES, CH), bf16),
            pltpu.VMEM((1, CLASSES), f32),
            pltpu.SMEM((n, 3), jnp.int32),
            pltpu.SMEM((subs, tiles), jnp.int32),
            dma((n,)),
            dma((10,)),
            dma((folds - 1, n, 3)),
            dma((folds - 1, n, 3)),
            dma((n, 3)),
            dma((n, 3)),
            dma((n, 3)),
            dma((n, 3)),
            dma((n,)),
            dma((n,)),
            dma((folds,)),
            dma((folds,)),
            dma((3,)),
            dma((3,)),
        ],
        compiler_params=pltpu.CompilerParams(
            collective_id=0, has_side_effects=True, vmem_limit_bytes=56 * 1024 * 1024
        ),
    )(
        features.reshape(n, ROWS, in_width),
        taps_first.swapaxes(-1, -2).reshape(27 * CH, cin),
        gf,
        sf,
        taps_second.reshape(27 * CH, CH),
        gs,
        ss,
        hw.T,
        hb,
        corners,
        counts.T,
    )


def place_kernel(own, sib, tail, tail_sib, direct, meta, out, rows, sems):
    n = own.shape[0]
    fold, sub, tile = (lax.axis_index(a) for a in ("folds", "sub", "tiles"))
    folds, subs = lax.axis_size("folds"), lax.axis_size("sub")
    span = out.shape[0]
    edge = min(span, WE - span)
    lane_y = lax.shift_right_logical(iota((TZ, LANES), 1), 4)
    depth = iota((TZ, LANES), 0)
    x0 = (fold * subs + sub) * span
    base = (1 - sub) * (WE - span)
    masks = {}
    for k in range(4):
        for w in range(n):
            cz, cx, cy = (
                jnp.concatenate([meta[k, 3 * w + c : 3 * w + c + 1, :].astype(jnp.int32)] * (LANES // 128), axis=1)
                for c in range(3)
            )
            inside = (lane_y >= cy) & (lane_y < cy + WE)
            deep = (depth >= cz) if k < 2 else ((depth < cz) & (tile > 0))
            masks[k, w] = inside & deep, cx[:, :WCLS]
    begin = jnp.where(sub == 0, WE - edge, 0)
    places = [(edge + m, None) for m in range(span - edge)] + [(begin + e, e) for e in range(edge)]
    copies = []
    for r, (position, e) in enumerate(places):
        i = position - base
        x = x0 + i
        total = jnp.zeros((TZ, LANES), f32)
        for k, ref in enumerate((own, sib, tail, tail_sib)):
            for w in range(n):
                if k == 2 and w == n - 1 and e is not None:
                    part = direct[0, e].astype(f32)
                    for d in range(1, folds):
                        part = part + direct[d, e].astype(f32)
                else:
                    part = ref[w, position].astype(f32)
                mask, cx = masks[k, w]
                part = jnp.where((cx <= x) & (x < cx + WE), part, 0.0)
                wide = jnp.concatenate([part] * -(-LANES // WCLS), axis=1)[:, :LANES]
                total = total + jnp.where(mask, wide, 0.0)
        rows[r] = total
        copy = pltpu.make_async_copy(rows.at[r], out.at[i], sems.at[r])
        copy.start()
        copies.append(copy)
    for copy in copies:
        copy.wait()


def place(*blocks):
    span = VX // (lax.axis_size("folds") * lax.axis_size("sub"))
    vmem = pl.BlockSpec(memory_space=pltpu.VMEM)
    return pl.pallas_call(
        place_kernel,
        out_shape=jax.ShapeDtypeStruct((span, TZ, LANES), f32),
        in_specs=[vmem] * 6,
        out_specs=pl.BlockSpec(memory_space=pltpu.HBM),
        scratch_shapes=[pltpu.VMEM((span, TZ, LANES), f32), pltpu.SemaphoreType.DMA((span,))],
        compiler_params=pltpu.CompilerParams(vmem_limit_bytes=12 * 1024 * 1024),
    )(*blocks)


def on_device(features, conv_one, gain_one, shift_one, conv_two, gain_two, shift_two, head_weight, head_bias, corners, counts):
    blocks = decode_send(
        features[0], conv_one[0], gain_one, shift_one, conv_two[0], gain_two, shift_two,
        head_weight[0], head_bias, corners, counts,
    )
    return place(*blocks).transpose(1, 0, 2)


def solution(mesh):
    windows = ("groups", "tiles", "sub")
    placed = (
        P("folds", windows, None, None, None),
        P("folds", None, None, None, None, None),
        P("folds", None),
        P("folds", None),
        P("folds", None, None, None, None, None),
        P("folds", None),
        P("folds", None),
        P("folds", None, None),
        P("folds", None),
        P(windows, None),
        P("groups", None),
    )
    return jax.shard_map(
        on_device,
        mesh=mesh,
        in_specs=placed,
        out_specs=P(("groups", "tiles"), ("folds", "sub"), None),
        check_vma=False,
    )
```

```python
import jax
import jax.numpy as jnp
from jax import lax
from jax.experimental import pallas as pl
from jax.experimental.pallas import tpu as pltpu
from jax.sharding import PartitionSpec as P

CH = 32
CLASSES = 16
WE = 16
TZ = 16
VX = 40
VY = 40
ROWS = WE * WE
WIDTH = WE * CH
WCLS = WE * CLASSES
LANES = VY * CLASSES

epsilon = 1e-05
leak_slope = 0.01

f32 = jnp.float32
bf16 = jnp.bfloat16
MESH = pl.DeviceIdType.MESH


def iota(shape, dim):
    return lax.broadcasted_iota(jnp.int32, shape, dim)


def one_hot(mask):
    return jnp.where(mask, 1.0, 0.0)


def spread_lanes(vec, width):
    n = vec.shape[1]
    pick = one_hot(iota((n, width), 0) == iota((n, width), 1) % n)
    return jnp.dot(vec, pick, precision=lax.Precision.HIGHEST, preferred_element_type=f32)


def build_first(taps_ref, band):
    cin = taps_ref.shape[1]
    pick = one_hot(iota((cin, 2 * cin), 0) == iota((cin, 2 * cin), 1) % cin).astype(bf16)
    twice = jnp.dot(taps_ref[...], pick, preferred_element_type=f32)
    low = iota((CH, 2 * cin), 1) < cin
    none = jnp.zeros((CH, 2 * cin), f32)
    blank = jnp.zeros((2 * CH, 4 * cin), bf16)
    for dz in range(3):
        groups, wrap = [], []
        for dx in range(3):
            first = (dz * 3 + dx) * 3 * CH
            t0, t1, t2 = (twice[first + dy * CH : first + (dy + 1) * CH] for dy in range(3))
            t01 = jnp.where(low, t0, t1)
            t12 = jnp.where(low, t1, t2)
            lower = jnp.concatenate([t01, jnp.where(low, t2, none)], axis=1)
            upper = jnp.concatenate([jnp.where(low, none, t0), t12], axis=1)
            groups.append(jnp.concatenate([lower, upper], axis=0).astype(bf16))
            lower = jnp.concatenate([t01, none], axis=1)
            upper = jnp.concatenate([none, t12], axis=1)
            wrap.append(jnp.concatenate([lower, upper], axis=0).astype(bf16))
        lanes = slice(dz * 4 * cin, (dz + 1) * 4 * cin)
        band[0, :, lanes] = jnp.concatenate([groups[1], groups[0], groups[2], blank], axis=0)
        band[1, :, lanes] = jnp.concatenate([groups[0], groups[1], blank, groups[2]], axis=0)
        band[2, :, lanes] = jnp.concatenate([wrap[0], wrap[1], blank, wrap[2]], axis=0)


def build_second(taps_ref, band):
    pick = one_hot(iota((CH, 4 * CH), 0) == iota((CH, 4 * CH), 1) % CH).astype(bf16)
    spread = jnp.dot(taps_ref[...], pick, preferred_element_type=f32)
    group = iota((4 * CH, 4 * CH), 1) // CH
    none = jnp.zeros((CH, 4 * CH), f32)
    blank = jnp.zeros((4 * CH, 4 * CH), f32)
    for dz in range(3):
        slab = {}
        for dx in range(3):
            first = (dz * 3 + dx) * 3 * CH
            taps = spread[first : first + 3 * CH]
            slab[dx, 0] = jnp.concatenate([taps, none], axis=0)
            slab[dx, 1] = jnp.concatenate([none, taps], axis=0)

        def columns(*which):
            out = blank
            for g, key in enumerate(which):
                if key is not None:
                    out = jnp.where(group == g, slab[key], out)
            return out.astype(bf16)

        rows = slice(dz * 4 * CH, (dz + 1) * 4 * CH)
        band[0, rows, : 4 * CH] = columns((1, 0), (1, 1), (0, 0), (0, 1))
        band[0, rows, 4 * CH :] = columns((2, 0), (2, 1), None, None)
        band[1, rows, : 4 * CH] = columns((0, 0), (0, 1), (1, 0), (1, 1))
        band[1, rows, 4 * CH :] = columns(None, None, (2, 0), (2, 1))


def combine(even, odd):
    rows = even.shape[0]
    low = iota((rows, 128), 1) < 64
    across = iota((rows, 128), 0) % WE
    centre = jnp.where(low, even[:, :128], odd[:, :128])
    before = pltpu.roll(jnp.where(low, odd[:, :128], even[:, :128]), 64, 1)
    after = jnp.where(low, even[:, 128:], odd[:, 128:])
    return (
        centre
        + jnp.where(across == 0, 0.0, pltpu.roll(before, 1, 0))
        + jnp.where(across == WE - 1, 0.0, pltpu.roll(after, rows - 1, 0))
    )


def view_first(padded, w, b, step):
    out = []
    for dz in range(3):
        rows = slice(dz * WE, dz * WE + ROWS)
        if b < 7:
            out.append(padded[w, rows, b * step : (b + 2) * step])
        else:
            out.append(padded[w, rows, 7 * step :])
            out.append(padded[w, rows, :step])
    return jnp.concatenate(out, axis=1)


def conv_first(padded, w, band, hidden, quarters):
    step = padded.shape[2] // 8
    for q in quarters:
        res = [
            lax.dot_general(
                view_first(padded, w, 2 * q + odd, step),
                band[kind],
                (((1,), (1,)), ((), ())),
                preferred_element_type=f32,
            )
            for odd, kind in ((0, 0), (1, 2 if q == 3 else 1))
        ]
        hidden[:, q * 128 : (q + 1) * 128] = combine(*res)


def conv_second(evens, odds, w, band, hidden, quarters):
    for q in quarters:
        res = [
            jnp.dot(
                jnp.concatenate(
                    [src[w, dz * WE : dz * WE + ROWS, q * 128 : (q + 1) * 128] for dz in range(3)], axis=1
                ),
                band[kind],
                preferred_element_type=f32,
            )
            for kind, src in enumerate((evens, odds))
        ]
        hidden[:, q * 128 : (q + 1) * 128] = combine(*res)


def over_voxels(row):
    row = row + pltpu.roll(row, 64, 1)
    return row + pltpu.roll(row, 32, 1)


def partial_sum(block):
    return jnp.sum(block.reshape(ROWS // 8, 8, 128), axis=0)


def statistics(hidden, gain):
    voxels = float(WE * WE * WE)
    about = over_voxels(hidden[:1, :128]) / 4.0
    first, square = None, None
    for q in range(4):
        off = hidden[:, q * 128 : (q + 1) * 128] - about
        parts = partial_sum(off), partial_sum(off * off)
        first = parts[0] if first is None else first + parts[0]
        square = parts[1] if square is None else square + parts[1]
    first = over_voxels(jnp.sum(first, axis=0, keepdims=True)) / voxels
    square = over_voxels(jnp.sum(square, axis=0, keepdims=True)) / voxels
    variance = jnp.maximum(square - first * first, 0.0)
    return about + first, lax.rsqrt(variance + epsilon) * gain


def normalize(hidden, stats, shift):
    mean_value, factor = stats
    out = []
    for q in range(4):
        scaled = (hidden[:, q * 128 : (q + 1) * 128] - mean_value) * factor + shift
        out.append(jnp.maximum(scaled, leak_slope * scaled))
    return out


def store_normed(values, evens, odds, w):
    rows = slice(WE, WE + ROWS)
    lane = iota((ROWS, 128), 1)
    low = lane < 64
    for q in range(4):
        even = values[q] if q < 3 else jnp.where(lane >= 96, 0.0, values[q])
        evens[w, rows, q * 128 : (q + 1) * 128] = even.astype(bf16)
        odd = pltpu.roll(jnp.where(low, values[(q + 1) % 4], values[q]), 64, 1)
        odd = odd if q < 3 else jnp.where(lane < 32, 0.0, odd)
        odds[w, rows, q * 128 : (q + 1) * 128] = odd.astype(bf16)


def bell(at):
    off = at.astype(f32) - (WE - 1) / 2.0
    return -(off * off) / (2.0 * (WE / 4.0) ** 2)


def prepare_head(corner, live, head_weight, placed, head, gauss):
    cz, cx, cy = corner
    row = iota((ROWS, 128), 0)
    lane = iota((ROWS, 128), 1)
    source = ((row - cz) & (WE - 1)) * WE + ((lax.shift_right_logical(row, 4) - cx) & (WE - 1))
    for half in range(2):
        lanes = slice(half * 128, (half + 1) * 128)
        placed[:, lanes] = one_hot(source == lane + half * 128).astype(bf16)
        z, x = lax.shift_right_logical(row, 4), row & (WE - 1)
        y = (lax.shift_right_logical(lane, 4) + half * 8 - cy) & (WE - 1)
        gauss[:, lanes] = jnp.where(live, jnp.exp(bell(z) + bell(x) + bell(y)), 0.0)
    at = lax.shift_right_logical(iota((CH, WCLS), 1), 4) - cy
    for u in range(WE):
        head[u * CH : (u + 1) * CH, :] = jnp.where(((at - u - 2) & (WE - 1)) == 0, head_weight, 0.0).astype(bf16)


def apply_head(values, placed, head, gauss, bias):
    second = jnp.concatenate([v.astype(bf16) for v in values], axis=1)
    logits = jnp.dot(second, head[...], preferred_element_type=f32) + bias
    weighted = (logits * gauss[...]).astype(bf16)
    return jnp.dot(placed[...], weighted, preferred_element_type=f32).astype(bf16)


def places_of(span, sub):
    edge = min(span, WE - span)
    begin = jnp.where(sub == 0, WE - edge, 0)
    base = (1 - sub) * (WE - span)
    positions = [edge + m for m in range(span - edge)] + [begin + e for e in range(edge)]
    return [(p, p - base) for p in positions]


def masks_of(meta, sources, tile):
    lane_y = lax.shift_right_logical(iota((TZ, LANES), 1), 4)
    depth = iota((TZ, LANES), 0)
    masks = {}
    for k, w in sources:
        cz, cx, cy = (
            jnp.concatenate([meta[k, 3 * w + c : 3 * w + c + 1, :].astype(jnp.int32)] * (LANES // 128), axis=1)
            for c in range(3)
        )
        inside = (lane_y >= cy) & (lane_y < cy + WE)
        deep = (depth >= cz) if k < 2 else ((depth < cz) & (tile > 0))
        masks[k, w] = inside & deep, cx[:, :WCLS]
    return masks


def masked(part, mask, x):
    zy, cx = mask
    part = jnp.where((cx <= x) & (x < cx + WE), part, 0.0)
    wide = jnp.concatenate([part] * -(-LANES // WCLS), axis=1)[:, :LANES]
    return jnp.where(zy, wide, 0.0)


def cut(kind, piece, first_id, count):
    first, size = piece
    out, at = [], 0
    for c in range(count):
        rows = -(-(size - at) // (count - c))
        if rows:
            out.append((kind, first + at, rows, first_id + c))
            at += rows
    return out


def decode_send_kernel(
    features, taps_first, gain_first, shift_first, taps_second, gain_second, shift_second,
    head_weight, head_bias, corners_in, counts_in,
    tail, tail_sib, meta, acc,
    own, sib, padded, evens, odds, band_first, band_second, hidden, ready, got, placed, head, gauss,
    taps_one, taps_two, gains, weights, biases, corners, counts,
    load_sems, in_sems, x_send, x_recv, s_send, s_recv, z_send, z_recv, f_send, f_recv, m_send, m_recv,
):
    n = padded.shape[0]
    fold, sub, tile = (lax.axis_index(a) for a in ("folds", "sub", "tiles"))
    folds, subs, tiles = (lax.axis_size(a) for a in ("folds", "sub", "tiles"))
    span = VX // (folds * subs)
    edge = min(span, WE - span)
    loads = [
        pltpu.make_async_copy(features.at[w], padded.at[w, WE : WE + ROWS, :], load_sems.at[w])
        for w in range(n)
    ]
    small = [
        pltpu.make_async_copy(src, dst, in_sems.at[k])
        for k, (src, dst) in enumerate(
            (
                (corners_in, corners),
                (counts_in, counts),
                (head_weight, weights),
                (taps_first, taps_one),
                (taps_second, taps_two),
                (head_bias, biases),
                (gain_first, gains.at[0]),
                (shift_first, gains.at[1]),
                (gain_second, gains.at[2]),
                (shift_second, gains.at[3]),
            )
        )
    ]
    loads[0].start()
    for copy in small:
        copy.start()
    for load in loads[1:]:
        load.start()

    barrier = pltpu.get_barrier_semaphore()
    other = 1 - sub
    later, earlier = lax.rem(tile + 1, tiles), lax.rem(tile + tiles - 1, tiles)

    def greet(**where):
        pl.semaphore_signal(barrier, inc=1, device_id=where, device_id_type=MESH)

    def greet_tile(at):
        greet(tiles=at)
        greet(tiles=at, sub=other)
        for d in range(1, folds):
            greet(tiles=at, folds=lax.rem(fold + d, folds))

    greet(sub=other)
    for d in range(1, folds):
        greet(folds=lax.rem(fold + d, folds))

    @pl.when(tile < tiles - 1)
    def _():
        greet_tile(tile + 1)

    @pl.when(tile > 0)
    def _():
        greet_tile(tile - 1)

    for w in range(n):
        for ref in (padded, evens, odds):
            ref[w, :WE, :] = jnp.zeros((WE, ref.shape[2]), bf16)
            ref[w, WE + ROWS :, :] = jnp.zeros((WE, ref.shape[2]), bf16)
    for copy in small[:3]:
        copy.wait()
    pick = one_hot(iota((CLASSES, WCLS), 0) == iota((CLASSES, WCLS), 1) % CLASSES)
    head_rows = lax.dot_general(
        weights[...], pick.astype(bf16), (((0,), (0,)), ((), ())), preferred_element_type=f32
    )
    live_count = counts[sub, tile]
    for w in range(n):
        corner = corners[w, 0], corners[w, 1], corners[w, 2]
        prepare_head(corner, w < live_count, head_rows, placed.at[w], head.at[w], gauss.at[w])
    row_id = iota((8, 128), 0)
    corner_rows = jnp.zeros((8, 128), f32)
    for w in range(n):
        for c in range(3):
            at = corners[w, c].astype(f32)
            at = at - (tile * TZ).astype(f32) if c == 0 else at
            corner_rows = jnp.where(row_id == 3 * w + c, at, corner_rows)
    meta[0] = corner_rows
    for copy in small[3:]:
        copy.wait()
    build_first(taps_one, band_first)
    build_second(taps_two, band_second)
    gain_one, shift_one, gain_two, shift_two = (spread_lanes(gains[k], 128) for k in range(4))
    bias = spread_lanes(biases[...], WCLS)

    theirs = (jnp.where(sub == 0, 0, WE - edge), edge)
    shared = (edge, WE - 2 * edge)
    mine = (jnp.where(sub == 0, WE - edge, 0), edge)
    shared_piece = [("shared", *shared, 0)] if 2 * span > WE else []
    whole = shared_piece + [("theirs", *theirs, 1), ("mine", *mine, 2)]
    order = [whole] * (n - 1) + [shared_piece + cut("theirs", theirs, 1, 2) + cut("mine", mine, 4, 3)]

    def start_of(f):
        return lax.rem(f * (subs * span) + span, WE)

    def remote(src, dst, sems, at, **where):
        return pltpu.make_async_remote_copy(
            src_ref=src, dst_ref=dst, send_sem=sems[0].at[at], recv_sem=sems[1].at[at],
            device_id=where, device_id_type=MESH,
        )

    x_copies, s_copies, z_copies, f_copies = {}, {}, {}, {}
    metas = [
        remote(meta.at[0], meta.at[1], (m_send, m_recv), 0, sub=other),
        remote(meta.at[0], meta.at[2], (m_send, m_recv), 1, tiles=later),
        remote(meta.at[0], meta.at[3], (m_send, m_recv), 2, tiles=later, sub=other),
    ]

    def norm_one(w):
        stats[w, 1] = statistics(hidden.at[w], gain_one)

    def store_one(w):
        store_normed(normalize(hidden.at[w], stats[w, 1], shift_one), evens, odds, w)

    def norm_two(w):
        stats[w, 2] = statistics(hidden.at[w], gain_two)

    def values_two(w):
        values[w] = normalize(hidden.at[w], stats[w, 2], shift_two)

    def finish(w):
        out = apply_head(values[w], placed.at[w], head.at[w], gauss.at[w], bias).reshape(WE, WE, WCLS)
        ready[w, :WE] = out
        ready[w, WE:] = out

    stats, values = {}, {}

    def send(w):
        if w == 0:
            near = folds

            @pl.when((tile == 0) | (tile == tiles - 1))
            def _():
                pl.semaphore_wait(barrier, near + folds + 1)

            @pl.when((tile > 0) & (tile < tiles - 1))
            def _():
                pl.semaphore_wait(barrier, near + 2 * (folds + 1))

        for _, first, size, at in order[w]:
            for d in range(1, folds):
                peer = lax.rem(fold + d, folds)
                copy = remote(
                    ready.at[w, pl.ds(start_of(peer) + first, size)],
                    got.at[d - 1, w, pl.ds(first, size)],
                    (x_send, x_recv), (d - 1, w, at), folds=peer,
                )
                copy.start()
                x_copies[d, w, at] = copy
        if w == 0:
            metas[0].start()

            @pl.when(tile < tiles - 1)
            def _():
                for copy in metas[1:]:
                    copy.start()

    def first(w, *quarters):
        conv_first(padded, w, band_first, hidden.at[w], quarters)

    def second(w, *quarters):
        conv_second(evens, odds, w, band_second, hidden.at[w], quarters)

    loads[0].wait()
    loads[1].wait()
    first(0, 0, 1, 2, 3)
    norm_one(0)
    first(1, 0, 1)
    store_one(0)
    second(0, 0, 1, 2, 3)
    first(1, 2, 3)
    norm_two(0)
    norm_one(1)
    values_two(0)
    finish(0)
    send(0)
    store_one(1)
    second(1, 0, 1, 2, 3)
    norm_two(1)
    values_two(1)
    finish(1)
    send(1)

    def gather(w, kind, first, size, at):
        rows = pl.ds(first, size)
        total = ready[w, pl.ds(start_of(fold) + first, size)].astype(f32)
        for d in range(1, folds):
            x_copies[d, w, at].wait_recv()
            total = total + got[d - 1, w, rows].astype(f32)
        own[w, rows] = total.astype(bf16)
        key = w, at
        if kind == "theirs":
            z_copies[key] = remote(
                own.at[w, rows], tail_sib.at[w, rows], (z_send, z_recv), key, tiles=later, sub=other
            )
        elif True:
            z_copies[key] = remote(own.at[w, rows], tail.at[w, rows], (z_send, z_recv), key, tiles=later)
        if key in z_copies:

            @pl.when(tile < tiles - 1)
            def _():
                z_copies[key].start()

        if kind != "mine":
            s_copies[key] = remote(own.at[w, rows], sib.at[w, rows], (s_send, s_recv), key, sub=other)
            s_copies[key].start()

    def forward(w):
        if shared_piece:
            rows = pl.ds(*shared)
            f_copies[w] = remote(tail.at[w, rows], tail_sib.at[w, rows], (f_send, f_recv), w, sub=other)

            @pl.when(tile > 0)
            def _():
                z_copies[w, 0].wait_recv()
                f_copies[w].start()

    for w in range(n - 1):
        for piece in order[w]:
            gather(w, *piece)
    last = n - 1
    early = [p for p in order[last] if p[0] != "mine"]
    for piece in early:
        gather(last, *piece)
    for w in range(n - 1):
        forward(w)
    for piece in order[last][len(early) :]:
        gather(last, *piece)

    metas[0].wait()
    for copy in s_copies.values():
        copy.wait()

    @pl.when(tile > 0)
    def _():
        for copy in metas[1:]:
            copy.wait_recv()
        for (w, at), copy in z_copies.items():
            if w < last and not (at == 0 and w in f_copies):
                copy.wait_recv()
        for copy in f_copies.values():
            copy.wait()

    refs = own, sib, tail, tail_sib
    sources = [(k, w) for k in range(4) for w in range(n) if k < 2 or w < last]
    masks = masks_of(meta, sources, tile)
    x0 = (fold * subs + sub) * span
    for r, (position, i) in enumerate(places_of(span, sub)):
        total = None
        for k, w in sources:
            part = masked(refs[k][w, position].astype(f32), masks[k, w], x0 + i)
            total = part if total is None else total + part
        acc[r] = total

    forward(last)

    @pl.when(tile > 0)
    def _():
        for (w, at), copy in z_copies.items():
            if w == last and not (at == 0 and w in f_copies):
                copy.wait_recv()
        if last in f_copies:
            f_copies[last].wait()

    for copy in x_copies.values():
        copy.wait_send()

    @pl.when(tile < tiles - 1)
    def _():
        for copy in metas[1:] + list(z_copies.values()):
            copy.wait_send()


def decode_send(features, taps_first, gf, sf, taps_second, gs, ss, hw, hb, corners, counts):
    n = features.shape[0]
    in_width = features.shape[-1]
    cin = in_width // WE
    folds, subs, tiles = (lax.axis_size(a) for a in ("folds", "sub", "tiles"))
    span = VX // (folds * subs)
    edge = min(span, WE - span)
    hbm = pl.BlockSpec(memory_space=pltpu.HBM)
    vmem = pl.BlockSpec(memory_space=pltpu.VMEM)
    dma = pltpu.SemaphoreType.DMA
    block = pltpu.VMEM((n, WE, WE, WCLS), bf16)
    return pl.pallas_call(
        decode_send_kernel,
        out_shape=[block, block, pltpu.VMEM((4, 8, 128), f32), pltpu.VMEM((span, TZ, LANES), f32)],
        in_specs=[hbm] * 11,
        out_specs=[vmem] * 4,
        scratch_shapes=[
            pltpu.VMEM((n, WE, WE, WCLS), bf16),
            pltpu.VMEM((n, WE, WE, WCLS), bf16),
            pltpu.VMEM((n, ROWS + 2 * WE, in_width), bf16),
            pltpu.VMEM((n, ROWS + 2 * WE, WIDTH), bf16),
            pltpu.VMEM((n, ROWS + 2 * WE, WIDTH), bf16),
            pltpu.VMEM((3, 8 * CH, 12 * cin), bf16),
            pltpu.VMEM((2, 12 * CH, 8 * CH), bf16),
            pltpu.VMEM((n, ROWS, WIDTH), f32),
            pltpu.VMEM((n, 2 * WE, WE, WCLS), bf16),
            pltpu.VMEM((folds - 1, n, WE, WE, WCLS), bf16),
            pltpu.VMEM((n, ROWS, ROWS), bf16),
            pltpu.VMEM((n, WIDTH, WCLS), bf16),
            pltpu.VMEM((n, ROWS, WCLS), f32),
            pltpu.VMEM((27 * CH, cin), bf16),
            pltpu.VMEM((27 * CH, CH), bf16),
            pltpu.VMEM((4, 1, CH), f32),
            pltpu.VMEM((CLASSES, CH), bf16),
            pltpu.VMEM((1, CLASSES), f32),
            pltpu.SMEM((n, 3), jnp.int32),
            pltpu.SMEM((subs, tiles), jnp.int32),
            dma((n,)),
            dma((10,)),
            dma((folds - 1, n, 8)),
            dma((folds - 1, n, 8)),
            dma((n, 8)),
            dma((n, 8)),
            dma((n, 8)),
            dma((n, 8)),
            dma((n,)),
            dma((n,)),
            dma((3,)),
            dma((3,)),
        ],
        compiler_params=pltpu.CompilerParams(
            collective_id=0, has_side_effects=True, vmem_limit_bytes=56 * 1024 * 1024
        ),
    )(
        features.reshape(n, ROWS, in_width),
        taps_first.swapaxes(-1, -2).reshape(27 * CH, cin),
        gf,
        sf,
        taps_second.reshape(27 * CH, CH),
        gs,
        ss,
        hw.T,
        hb,
        corners,
        counts.T,
    )


def place_kernel(tail, tail_sib, meta, acc, out, rows, sems):
    n = tail_sib.shape[0]
    fold, sub, tile = (lax.axis_index(a) for a in ("folds", "sub", "tiles"))
    folds, subs = lax.axis_size("folds"), lax.axis_size("sub")
    span = out.shape[0]
    x0 = (fold * subs + sub) * span
    w = n - 1
    masks = masks_of(meta, ((2, w), (3, w)), tile)
    copies = []
    for r, (position, i) in enumerate(places_of(span, sub)):
        part = tail[w, position].astype(f32)
        total = acc[r] + masked(part, masks[2, w], x0 + i)
        part = tail_sib[w, position].astype(f32)
        rows[r] = total + masked(part, masks[3, w], x0 + i)
        copy = pltpu.make_async_copy(rows.at[r], out.at[i], sems.at[r])
        copy.start()
        copies.append(copy)
    for copy in copies:
        copy.wait()


def place(*blocks):
    span = VX // (lax.axis_size("folds") * lax.axis_size("sub"))
    vmem = pl.BlockSpec(memory_space=pltpu.VMEM)
    return pl.pallas_call(
        place_kernel,
        out_shape=jax.ShapeDtypeStruct((span, TZ, LANES), f32),
        in_specs=[vmem] * 4,
        out_specs=pl.BlockSpec(memory_space=pltpu.HBM),
        scratch_shapes=[pltpu.VMEM((span, TZ, LANES), f32), pltpu.SemaphoreType.DMA((span,))],
        compiler_params=pltpu.CompilerParams(vmem_limit_bytes=12 * 1024 * 1024),
    )(*blocks)


def on_device(features, conv_one, gain_one, shift_one, conv_two, gain_two, shift_two, head_weight, head_bias, corners, counts):
    blocks = decode_send(
        features[0], conv_one[0], gain_one, shift_one, conv_two[0], gain_two, shift_two,
        head_weight[0], head_bias, corners, counts,
    )
    return place(*blocks).transpose(1, 0, 2)


def solution(mesh):
    windows = ("groups", "tiles", "sub")
    placed = (
        P("folds", windows, None, None, None),
        P("folds", None, None, None, None, None),
        P("folds", None),
        P("folds", None),
        P("folds", None, None, None, None, None),
        P("folds", None),
        P("folds", None),
        P("folds", None, None),
        P("folds", None),
        P(windows, None),
        P("groups", None),
    )
    return jax.shard_map(
        on_device,
        mesh=mesh,
        in_specs=placed,
        out_specs=P(("groups", "tiles"), ("folds", "sub"), None),
        check_vma=False,
    )
```

```python
import jax
import jax.numpy as jnp
from jax import lax
from jax.experimental import pallas as pl
from jax.experimental.pallas import tpu as pltpu
from jax.sharding import PartitionSpec as P

CH = 32
CLASSES = 16
WE = 16
TZ = 16
VX = 40
VY = 40
ROWS = WE * WE
WIDTH = WE * CH
WCLS = WE * CLASSES
LANES = VY * CLASSES

epsilon = 1e-05
leak_slope = 0.01

f32 = jnp.float32
bf16 = jnp.bfloat16
MESH = pl.DeviceIdType.MESH


def iota(shape, dim):
    return lax.broadcasted_iota(jnp.int32, shape, dim)


def one_hot(mask):
    return jnp.where(mask, 1.0, 0.0)


def spread_lanes(vec, width):
    n = vec.shape[1]
    pick = one_hot(iota((n, width), 0) == iota((n, width), 1) % n)
    return jnp.dot(vec, pick, precision=lax.Precision.HIGHEST, preferred_element_type=f32)


def build_first(taps_ref, band):
    cin = taps_ref.shape[1]
    pick = one_hot(iota((cin, 2 * cin), 0) == iota((cin, 2 * cin), 1) % cin).astype(bf16)
    twice = jnp.dot(taps_ref[...], pick, preferred_element_type=f32)
    low = iota((CH, 2 * cin), 1) < cin
    none = jnp.zeros((CH, 2 * cin), f32)
    blank = jnp.zeros((2 * CH, 4 * cin), bf16)
    for dz in range(3):
        groups, wrap = [], []
        for dx in range(3):
            first = (dz * 3 + dx) * 3 * CH
            t0, t1, t2 = (twice[first + dy * CH : first + (dy + 1) * CH] for dy in range(3))
            t01 = jnp.where(low, t0, t1)
            t12 = jnp.where(low, t1, t2)
            lower = jnp.concatenate([t01, jnp.where(low, t2, none)], axis=1)
            upper = jnp.concatenate([jnp.where(low, none, t0), t12], axis=1)
            groups.append(jnp.concatenate([lower, upper], axis=0).astype(bf16))
            lower = jnp.concatenate([t01, none], axis=1)
            upper = jnp.concatenate([none, t12], axis=1)
            wrap.append(jnp.concatenate([lower, upper], axis=0).astype(bf16))
        lanes = slice(dz * 4 * cin, (dz + 1) * 4 * cin)
        band[0, :, lanes] = jnp.concatenate([groups[1], groups[0], groups[2], blank], axis=0)
        band[1, :, lanes] = jnp.concatenate([groups[0], groups[1], blank, groups[2]], axis=0)
        band[2, :, lanes] = jnp.concatenate([wrap[0], wrap[1], blank, wrap[2]], axis=0)


def build_second(taps_ref, band):
    pick = one_hot(iota((CH, 4 * CH), 0) == iota((CH, 4 * CH), 1) % CH).astype(bf16)
    spread = jnp.dot(taps_ref[...], pick, preferred_element_type=f32)
    group = iota((4 * CH, 4 * CH), 1) // CH
    none = jnp.zeros((CH, 4 * CH), f32)
    blank = jnp.zeros((4 * CH, 4 * CH), f32)
    for dz in range(3):
        slab = {}
        for dx in range(3):
            first = (dz * 3 + dx) * 3 * CH
            taps = spread[first : first + 3 * CH]
            slab[dx, 0] = jnp.concatenate([taps, none], axis=0)
            slab[dx, 1] = jnp.concatenate([none, taps], axis=0)

        def columns(*which):
            out = blank
            for g, key in enumerate(which):
                if key is not None:
                    out = jnp.where(group == g, slab[key], out)
            return out.astype(bf16)

        rows = slice(dz * 4 * CH, (dz + 1) * 4 * CH)
        band[0, rows, : 4 * CH] = columns((1, 0), (1, 1), (0, 0), (0, 1))
        band[0, rows, 4 * CH :] = columns((2, 0), (2, 1), None, None)
        band[1, rows, : 4 * CH] = columns((0, 0), (0, 1), (1, 0), (1, 1))
        band[1, rows, 4 * CH :] = columns(None, None, (2, 0), (2, 1))


def combine(even, odd):
    rows = even.shape[0]
    low = iota((rows, 128), 1) < 64
    across = iota((rows, 128), 0) % WE
    centre = jnp.where(low, even[:, :128], odd[:, :128])
    before = pltpu.roll(jnp.where(low, odd[:, :128], even[:, :128]), 64, 1)
    after = jnp.where(low, even[:, 128:], odd[:, 128:])
    return (
        centre
        + jnp.where(across == 0, 0.0, pltpu.roll(before, 1, 0))
        + jnp.where(across == WE - 1, 0.0, pltpu.roll(after, rows - 1, 0))
    )


def view_first(padded, w, b, step):
    out = []
    for dz in range(3):
        rows = slice(dz * WE, dz * WE + ROWS)
        if b < 7:
            out.append(padded[w, rows, b * step : (b + 2) * step])
        else:
            out.append(padded[w, rows, 7 * step :])
            out.append(padded[w, rows, :step])
    return jnp.concatenate(out, axis=1)


def conv_first(padded, w, band, hidden, quarters):
    step = padded.shape[2] // 8
    for q in quarters:
        res = [
            lax.dot_general(
                view_first(padded, w, 2 * q + odd, step),
                band[kind],
                (((1,), (1,)), ((), ())),
                preferred_element_type=f32,
            )
            for odd, kind in ((0, 0), (1, 2 if q == 3 else 1))
        ]
        hidden[:, q * 128 : (q + 1) * 128] = combine(*res)


def conv_second(evens, odds, w, band, hidden, quarters):
    for q in quarters:
        res = [
            jnp.dot(
                jnp.concatenate(
                    [src[w, dz * WE : dz * WE + ROWS, q * 128 : (q + 1) * 128] for dz in range(3)], axis=1
                ),
                band[kind],
                preferred_element_type=f32,
            )
            for kind, src in enumerate((evens, odds))
        ]
        hidden[:, q * 128 : (q + 1) * 128] = combine(*res)


def over_voxels(row):
    row = row + pltpu.roll(row, 64, 1)
    return row + pltpu.roll(row, 32, 1)


def partial_sum(block):
    return jnp.sum(block.reshape(ROWS // 8, 8, 128), axis=0)


def statistics(hidden, gain):
    voxels = float(WE * WE * WE)
    about = over_voxels(hidden[:1, :128]) / 4.0
    first, square = None, None
    for q in range(4):
        off = hidden[:, q * 128 : (q + 1) * 128] - about
        parts = partial_sum(off), partial_sum(off * off)
        first = parts[0] if first is None else first + parts[0]
        square = parts[1] if square is None else square + parts[1]
    first = over_voxels(jnp.sum(first, axis=0, keepdims=True)) / voxels
    square = over_voxels(jnp.sum(square, axis=0, keepdims=True)) / voxels
    variance = jnp.maximum(square - first * first, 0.0)
    return about + first, lax.rsqrt(variance + epsilon) * gain


def normalize(hidden, stats, shift):
    mean_value, factor = stats
    out = []
    for q in range(4):
        scaled = (hidden[:, q * 128 : (q + 1) * 128] - mean_value) * factor + shift
        out.append(jnp.maximum(scaled, leak_slope * scaled))
    return out


def store_normed(values, evens, odds, w):
    rows = slice(WE, WE + ROWS)
    lane = iota((ROWS, 128), 1)
    low = lane < 64
    for q in range(4):
        even = values[q] if q < 3 else jnp.where(lane >= 96, 0.0, values[q])
        evens[w, rows, q * 128 : (q + 1) * 128] = even.astype(bf16)
        odd = pltpu.roll(jnp.where(low, values[(q + 1) % 4], values[q]), 64, 1)
        odd = odd if q < 3 else jnp.where(lane < 32, 0.0, odd)
        odds[w, rows, q * 128 : (q + 1) * 128] = odd.astype(bf16)


def bell(at):
    off = at.astype(f32) - (WE - 1) / 2.0
    return -(off * off) / (2.0 * (WE / 4.0) ** 2)


def prepare_head(corner, live, head_weight, placed, head, gauss):
    cz, cx, cy = corner
    row = iota((ROWS, 128), 0)
    lane = iota((ROWS, 128), 1)
    source = ((row - cz) & (WE - 1)) * WE + ((lax.shift_right_logical(row, 4) - cx) & (WE - 1))
    for half in range(2):
        lanes = slice(half * 128, (half + 1) * 128)
        placed[:, lanes] = one_hot(source == lane + half * 128).astype(bf16)
        z, x = lax.shift_right_logical(row, 4), row & (WE - 1)
        y = (lax.shift_right_logical(lane, 4) + half * 8 - cy) & (WE - 1)
        gauss[:, lanes] = jnp.where(live, jnp.exp(bell(z) + bell(x) + bell(y)), 0.0)
    at = lax.shift_right_logical(iota((CH, WCLS), 1), 4) - cy
    for u in range(WE):
        head[u * CH : (u + 1) * CH, :] = jnp.where(((at - u - 2) & (WE - 1)) == 0, head_weight, 0.0).astype(bf16)


def apply_head(values, placed, head, gauss, bias):
    second = jnp.concatenate([v.astype(bf16) for v in values], axis=1)
    logits = jnp.dot(second, head[...], preferred_element_type=f32) + bias
    weighted = (logits * gauss[...]).astype(bf16)
    return jnp.dot(placed[...], weighted, preferred_element_type=f32).astype(bf16)


def places_of(span, sub):
    edge = min(span, WE - span)
    begin = jnp.where(sub == 0, WE - edge, 0)
    base = (1 - sub) * (WE - span)
    positions = [edge + m for m in range(span - edge)] + [begin + e for e in range(edge)]
    return [(p, p - base) for p in positions]


def masks_of(meta, sources, tile):
    lane_y = lax.shift_right_logical(iota((TZ, LANES), 1), 4)
    depth = iota((TZ, LANES), 0)
    masks = {}
    for k, w in sources:
        cz, cx, cy = (
            jnp.concatenate([meta[k, 3 * w + c : 3 * w + c + 1, :].astype(jnp.int32)] * (LANES // 128), axis=1)
            for c in range(3)
        )
        inside = (lane_y >= cy) & (lane_y < cy + WE)
        deep = (depth >= cz) if k < 2 else ((depth < cz) & (tile > 0))
        masks[k, w] = inside & deep, cx[:, :WCLS]
    return masks


def masked(part, mask, x):
    zy, cx = mask
    part = jnp.where((cx <= x) & (x < cx + WE), part, 0.0)
    wide = jnp.concatenate([part] * -(-LANES // WCLS), axis=1)[:, :LANES]
    return jnp.where(zy, wide, 0.0)


def cut(kind, piece, first_id, count):
    first, size = piece
    out, at = [], 0
    for c in range(count):
        rows = -(-(size - at) // (count - c))
        if rows:
            out.append((kind, first + at, rows, first_id + c))
            at += rows
    return out


def decode_send_kernel(
    features, taps_first, gain_first, shift_first, taps_second, gain_second, shift_second,
    head_weight, head_bias, corners_in, counts_in,
    tail, tail_sib, meta, acc,
    own, sib, padded, evens, odds, band_first, band_second, hidden, ready, got, placed, head, gauss,
    taps_one, taps_two, gains, weights, biases, corners, counts,
    load_sems, in_sems, x_send, x_recv, s_send, s_recv, z_send, z_recv, f_send, f_recv, m_send, m_recv,
):
    n = padded.shape[0]
    fold, sub, tile = (lax.axis_index(a) for a in ("folds", "sub", "tiles"))
    folds, subs, tiles = (lax.axis_size(a) for a in ("folds", "sub", "tiles"))
    span = VX // (folds * subs)
    edge = min(span, WE - span)
    loads = [
        pltpu.make_async_copy(features.at[w], padded.at[w, WE : WE + ROWS, :], load_sems.at[w])
        for w in range(n)
    ]
    small = [
        pltpu.make_async_copy(src, dst, in_sems.at[k])
        for k, (src, dst) in enumerate(
            (
                (corners_in, corners),
                (counts_in, counts),
                (head_weight, weights),
                (taps_first, taps_one),
                (taps_second, taps_two),
                (head_bias, biases),
                (gain_first, gains.at[0]),
                (shift_first, gains.at[1]),
                (gain_second, gains.at[2]),
                (shift_second, gains.at[3]),
            )
        )
    ]
    loads[0].start()
    for copy in small:
        copy.start()
    for load in loads[1:]:
        load.start()

    barrier = pltpu.get_barrier_semaphore()
    other = 1 - sub
    later, earlier = lax.rem(tile + 1, tiles), lax.rem(tile + tiles - 1, tiles)

    def greet(**where):
        pl.semaphore_signal(barrier, inc=1, device_id=where, device_id_type=MESH)

    def greet_tile(at):
        greet(tiles=at)
        greet(tiles=at, sub=other)
        for d in range(1, folds):
            greet(tiles=at, folds=lax.rem(fold + d, folds))

    greet(sub=other)
    for d in range(1, folds):
        greet(folds=lax.rem(fold + d, folds))

    @pl.when(tile < tiles - 1)
    def _():
        greet_tile(tile + 1)

    @pl.when(tile > 0)
    def _():
        greet_tile(tile - 1)

    for w in range(n):
        for ref in (padded, evens, odds):
            ref[w, :WE, :] = jnp.zeros((WE, ref.shape[2]), bf16)
            ref[w, WE + ROWS :, :] = jnp.zeros((WE, ref.shape[2]), bf16)
    for copy in small[:3]:
        copy.wait()
    pick = one_hot(iota((CLASSES, WCLS), 0) == iota((CLASSES, WCLS), 1) % CLASSES)
    head_rows = lax.dot_general(
        weights[...], pick.astype(bf16), (((0,), (0,)), ((), ())), preferred_element_type=f32
    )
    live_count = counts[sub, tile]
    for w in range(n):
        corner = corners[w, 0], corners[w, 1], corners[w, 2]
        prepare_head(corner, w < live_count, head_rows, placed.at[w], head.at[w], gauss.at[w])
    row_id = iota((8, 128), 0)
    corner_rows = jnp.zeros((8, 128), f32)
    for w in range(n):
        for c in range(3):
            at = corners[w, c].astype(f32)
            at = at - (tile * TZ).astype(f32) if c == 0 else at
            corner_rows = jnp.where(row_id == 3 * w + c, at, corner_rows)
    meta[0] = corner_rows
    for copy in small[3:]:
        copy.wait()
    build_first(taps_one, band_first)
    build_second(taps_two, band_second)
    gain_one, shift_one, gain_two, shift_two = (spread_lanes(gains[k], 128) for k in range(4))
    bias = spread_lanes(biases[...], WCLS)

    theirs = (jnp.where(sub == 0, 0, WE - edge), edge)
    shared = (edge, WE - 2 * edge)
    mine = (jnp.where(sub == 0, WE - edge, 0), edge)
    shared_piece = [("shared", *shared, 0)] if 2 * span > WE else []
    whole = shared_piece + [("theirs", *theirs, 1), ("mine", *mine, 2)]
    order = [whole] * (n - 1) + [shared_piece + cut("theirs", theirs, 1, 2) + cut("mine", mine, 4, 3)]

    def start_of(f):
        return lax.rem(f * (subs * span) + span, WE)

    def remote(src, dst, sems, at, **where):
        return pltpu.make_async_remote_copy(
            src_ref=src, dst_ref=dst, send_sem=sems[0].at[at], recv_sem=sems[1].at[at],
            device_id=where, device_id_type=MESH,
        )

    x_copies, s_copies, z_copies, f_copies = {}, {}, {}, {}
    metas = [
        remote(meta.at[0], meta.at[1], (m_send, m_recv), 0, sub=other),
        remote(meta.at[0], meta.at[2], (m_send, m_recv), 1, tiles=later),
        remote(meta.at[0], meta.at[3], (m_send, m_recv), 2, tiles=later, sub=other),
    ]

    def norm_one(w):
        stats[w, 1] = statistics(hidden.at[w], gain_one)

    def store_one(w):
        store_normed(normalize(hidden.at[w], stats[w, 1], shift_one), evens, odds, w)

    def norm_two(w):
        stats[w, 2] = statistics(hidden.at[w], gain_two)

    def values_two(w):
        values[w] = normalize(hidden.at[w], stats[w, 2], shift_two)

    def finish(w):
        out = apply_head(values[w], placed.at[w], head.at[w], gauss.at[w], bias).reshape(WE, WE, WCLS)
        ready[w, :WE] = out
        ready[w, WE:] = out

    stats, values = {}, {}

    def send(w):
        if w == 0:
            neighbours = (tile + tiles - 1) // tiles + (2 * tiles - 2 - tile) // tiles
            pl.semaphore_wait(barrier, folds + neighbours * (folds + 1))

        for _, first, size, at in order[w]:
            for d in range(1, folds):
                peer = lax.rem(fold + d, folds)
                copy = remote(
                    ready.at[w, pl.ds(start_of(peer) + first, size)],
                    got.at[d - 1, w, pl.ds(first, size)],
                    (x_send, x_recv), (d - 1, w, at), folds=peer,
                )
                copy.start()
                x_copies[d, w, at] = copy
        if w == 0:
            metas[0].start()

            @pl.when(tile < tiles - 1)
            def _():
                for copy in metas[1:]:
                    copy.start()

    def first(w, *quarters):
        conv_first(padded, w, band_first, hidden.at[w], quarters)

    def second(w, *quarters):
        conv_second(evens, odds, w, band_second, hidden.at[w], quarters)

    loads[0].wait()
    loads[1].wait()
    first(0, 0, 1, 2, 3)
    norm_one(0)
    store_one(0)
    second(0, 0, 1, 2, 3)
    norm_two(0)
    values_two(0)
    finish(0)
    send(0)
    first(1, 0, 1, 2, 3)
    norm_one(1)
    store_one(1)
    second(1, 0, 1, 2, 3)
    norm_two(1)
    values_two(1)
    finish(1)
    send(1)

    def gather(w, kind, first, size, at):
        rows = pl.ds(first, size)
        total = ready[w, pl.ds(start_of(fold) + first, size)].astype(f32)
        for d in range(1, folds):
            x_copies[d, w, at].wait_recv()
            total = total + got[d - 1, w, rows].astype(f32)
        own[w, rows] = total.astype(bf16)
        key = w, at
        if kind == "theirs":
            z_copies[key] = remote(
                own.at[w, rows], tail_sib.at[w, rows], (z_send, z_recv), key, tiles=later, sub=other
            )
        elif True:
            z_copies[key] = remote(own.at[w, rows], tail.at[w, rows], (z_send, z_recv), key, tiles=later)
        if key in z_copies:

            @pl.when(tile < tiles - 1)
            def _():
                z_copies[key].start()

        if kind != "mine":
            s_copies[key] = remote(own.at[w, rows], sib.at[w, rows], (s_send, s_recv), key, sub=other)
            s_copies[key].start()

    def forward(w):
        if shared_piece:
            rows = pl.ds(*shared)
            f_copies[w] = remote(tail.at[w, rows], tail_sib.at[w, rows], (f_send, f_recv), w, sub=other)

            @pl.when(tile > 0)
            def _():
                z_copies[w, 0].wait_recv()
                f_copies[w].start()

    for w in range(n - 1):
        for piece in order[w]:
            gather(w, *piece)
    last = n - 1
    early = [p for p in order[last] if p[0] != "mine"]
    for piece in early:
        gather(last, *piece)
    for w in range(n - 1):
        forward(w)
    x0 = (fold * subs + sub) * span
    refs = own, sib, tail, tail_sib

    def accumulate(sources, fresh):
        masks = masks_of(meta, sources, tile)
        for r, (position, i) in enumerate(places_of(span, sub)):
            total = None if fresh else acc[r]
            for k, w in sources:
                part = masked(refs[k][w, position].astype(f32), masks[k, w], x0 + i)
                total = part if total is None else total + part
            acc[r] = total

    metas[0].wait()
    for (w, _), copy in s_copies.items():
        if w < last:
            copy.wait()

    accumulate([(k, w) for k in range(2) for w in range(last)], True)
    for piece in order[last][len(early) :]:
        gather(last, *piece)

    @pl.when(tile > 0)
    def _():
        for copy in metas[1:]:
            copy.wait_recv()
        for (w, at), copy in z_copies.items():
            if w < last and not (at == 0 and w in f_copies):
                copy.wait_recv()
        for copy in f_copies.values():
            copy.wait()

    for (w, _), copy in s_copies.items():
        if w == last:
            copy.wait()
    accumulate([(k, w) for k in (2, 3) for w in range(last)] + [(0, last), (1, last)], False)

    forward(last)

    @pl.when(tile > 0)
    def _():
        for (w, at), copy in z_copies.items():
            if w == last and not (at == 0 and w in f_copies):
                copy.wait_recv()
        if last in f_copies:
            f_copies[last].wait()

    for copy in x_copies.values():
        copy.wait_send()

    @pl.when(tile < tiles - 1)
    def _():
        for copy in metas[1:] + list(z_copies.values()):
            copy.wait_send()


def decode_send(features, taps_first, gf, sf, taps_second, gs, ss, hw, hb, corners, counts):
    n = features.shape[0]
    in_width = features.shape[-1]
    cin = in_width // WE
    folds, subs, tiles = (lax.axis_size(a) for a in ("folds", "sub", "tiles"))
    span = VX // (folds * subs)
    edge = min(span, WE - span)
    hbm = pl.BlockSpec(memory_space=pltpu.HBM)
    vmem = pl.BlockSpec(memory_space=pltpu.VMEM)
    dma = pltpu.SemaphoreType.DMA
    block = pltpu.VMEM((n, WE, WE, WCLS), bf16)
    return pl.pallas_call(
        decode_send_kernel,
        out_shape=[block, block, pltpu.VMEM((4, 8, 128), f32), pltpu.VMEM((span, TZ, LANES), f32)],
        in_specs=[hbm] * 11,
        out_specs=[vmem] * 4,
        scratch_shapes=[
            pltpu.VMEM((n, WE, WE, WCLS), bf16),
            pltpu.VMEM((n, WE, WE, WCLS), bf16),
            pltpu.VMEM((n, ROWS + 2 * WE, in_width), bf16),
            pltpu.VMEM((n, ROWS + 2 * WE, WIDTH), bf16),
            pltpu.VMEM((n, ROWS + 2 * WE, WIDTH), bf16),
            pltpu.VMEM((3, 8 * CH, 12 * cin), bf16),
            pltpu.VMEM((2, 12 * CH, 8 * CH), bf16),
            pltpu.VMEM((n, ROWS, WIDTH), f32),
            pltpu.VMEM((n, 2 * WE, WE, WCLS), bf16),
            pltpu.VMEM((folds - 1, n, WE, WE, WCLS), bf16),
            pltpu.VMEM((n, ROWS, ROWS), bf16),
            pltpu.VMEM((n, WIDTH, WCLS), bf16),
            pltpu.VMEM((n, ROWS, WCLS), f32),
            pltpu.VMEM((27 * CH, cin), bf16),
            pltpu.VMEM((27 * CH, CH), bf16),
            pltpu.VMEM((4, 1, CH), f32),
            pltpu.VMEM((CLASSES, CH), bf16),
            pltpu.VMEM((1, CLASSES), f32),
            pltpu.SMEM((n, 3), jnp.int32),
            pltpu.SMEM((subs, tiles), jnp.int32),
            dma((n,)),
            dma((10,)),
            dma((folds - 1, n, 8)),
            dma((folds - 1, n, 8)),
            dma((n, 8)),
            dma((n, 8)),
            dma((n, 8)),
            dma((n, 8)),
            dma((n,)),
            dma((n,)),
            dma((3,)),
            dma((3,)),
        ],
        compiler_params=pltpu.CompilerParams(
            collective_id=0, has_side_effects=True, vmem_limit_bytes=56 * 1024 * 1024
        ),
    )(
        features.reshape(n, ROWS, in_width),
        taps_first.swapaxes(-1, -2).reshape(27 * CH, cin),
        gf,
        sf,
        taps_second.reshape(27 * CH, CH),
        gs,
        ss,
        hw.T,
        hb,
        corners,
        counts.T,
    )


def place_kernel(tail, tail_sib, meta, acc, out, rows, sems):
    n = tail_sib.shape[0]
    fold, sub, tile = (lax.axis_index(a) for a in ("folds", "sub", "tiles"))
    folds, subs = lax.axis_size("folds"), lax.axis_size("sub")
    span = out.shape[0]
    x0 = (fold * subs + sub) * span
    w = n - 1
    masks = masks_of(meta, ((2, w), (3, w)), tile)
    copies = []
    for r, (position, i) in enumerate(places_of(span, sub)):
        part = tail[w, position].astype(f32)
        total = acc[r] + masked(part, masks[2, w], x0 + i)
        part = tail_sib[w, position].astype(f32)
        rows[r] = total + masked(part, masks[3, w], x0 + i)
        copy = pltpu.make_async_copy(rows.at[r], out.at[i], sems.at[r])
        copy.start()
        copies.append(copy)
    for copy in copies:
        copy.wait()


def place(*blocks):
    span = VX // (lax.axis_size("folds") * lax.axis_size("sub"))
    vmem = pl.BlockSpec(memory_space=pltpu.VMEM)
    return pl.pallas_call(
        place_kernel,
        out_shape=jax.ShapeDtypeStruct((span, TZ, LANES), f32),
        in_specs=[vmem] * 4,
        out_specs=pl.BlockSpec(memory_space=pltpu.HBM),
        scratch_shapes=[pltpu.VMEM((span, TZ, LANES), f32), pltpu.SemaphoreType.DMA((span,))],
        compiler_params=pltpu.CompilerParams(vmem_limit_bytes=12 * 1024 * 1024),
    )(*blocks)


def on_device(features, conv_one, gain_one, shift_one, conv_two, gain_two, shift_two, head_weight, head_bias, corners, counts):
    blocks = decode_send(
        features[0], conv_one[0], gain_one, shift_one, conv_two[0], gain_two, shift_two,
        head_weight[0], head_bias, corners, counts,
    )
    return place(*blocks).transpose(1, 0, 2)


def solution(mesh):
    windows = ("groups", "tiles", "sub")
    placed = (
        P("folds", windows, None, None, None),
        P("folds", None, None, None, None, None),
        P("folds", None),
        P("folds", None),
        P("folds", None, None, None, None, None),
        P("folds", None),
        P("folds", None),
        P("folds", None, None),
        P("folds", None),
        P(windows, None),
        P("groups", None),
    )
    return jax.shard_map(
        on_device,
        mesh=mesh,
        in_specs=placed,
        out_specs=P(("groups", "tiles"), ("folds", "sub"), None),
        check_vma=False,
    )
```

```python
import jax
import jax.numpy as jnp
from jax import lax
from jax.experimental import pallas as pl
from jax.experimental.pallas import tpu as pltpu
from jax.sharding import PartitionSpec as P

CH = 32
CLASSES = 16
WE = 16
TZ = 16
VX = 40
VY = 40
ROWS = WE * WE
WIDTH = WE * CH
WCLS = WE * CLASSES
LANES = VY * CLASSES

epsilon = 1e-05
leak_slope = 0.01

f32 = jnp.float32
bf16 = jnp.bfloat16
MESH = pl.DeviceIdType.MESH


def iota(shape, dim):
    return lax.broadcasted_iota(jnp.int32, shape, dim)


def one_hot(mask):
    return jnp.where(mask, 1.0, 0.0)


def spread_lanes(vec, width):
    n = vec.shape[1]
    pick = one_hot(iota((n, width), 0) == iota((n, width), 1) % n)
    return jnp.dot(vec, pick, precision=lax.Precision.HIGHEST, preferred_element_type=f32)


def build_first(taps_ref, band):
    cin = taps_ref.shape[1]
    pick = one_hot(iota((cin, 2 * cin), 0) == iota((cin, 2 * cin), 1) % cin).astype(bf16)
    twice = jnp.dot(taps_ref[...], pick, preferred_element_type=f32)
    low = iota((CH, 2 * cin), 1) < cin
    none = jnp.zeros((CH, 2 * cin), f32)
    blank = jnp.zeros((2 * CH, 4 * cin), bf16)
    for dz in range(3):
        groups, wrap = [], []
        for dx in range(3):
            first = (dz * 3 + dx) * 3 * CH
            t0, t1, t2 = (twice[first + dy * CH : first + (dy + 1) * CH] for dy in range(3))
            t01 = jnp.where(low, t0, t1)
            t12 = jnp.where(low, t1, t2)
            lower = jnp.concatenate([t01, jnp.where(low, t2, none)], axis=1)
            upper = jnp.concatenate([jnp.where(low, none, t0), t12], axis=1)
            groups.append(jnp.concatenate([lower, upper], axis=0).astype(bf16))
            lower = jnp.concatenate([t01, none], axis=1)
            upper = jnp.concatenate([none, t12], axis=1)
            wrap.append(jnp.concatenate([lower, upper], axis=0).astype(bf16))
        lanes = slice(dz * 4 * cin, (dz + 1) * 4 * cin)
        band[0, :, lanes] = jnp.concatenate([groups[1], groups[0], groups[2], blank], axis=0)
        band[1, :, lanes] = jnp.concatenate([groups[0], groups[1], blank, groups[2]], axis=0)
        band[2, :, lanes] = jnp.concatenate([wrap[0], wrap[1], blank, wrap[2]], axis=0)


def build_second(taps_ref, band):
    pick = one_hot(iota((CH, 4 * CH), 0) == iota((CH, 4 * CH), 1) % CH).astype(bf16)
    spread = jnp.dot(taps_ref[...], pick, preferred_element_type=f32)
    group = iota((4 * CH, 4 * CH), 1) // CH
    none = jnp.zeros((CH, 4 * CH), f32)
    blank = jnp.zeros((4 * CH, 4 * CH), f32)
    for dz in range(3):
        slab = {}
        for dx in range(3):
            first = (dz * 3 + dx) * 3 * CH
            taps = spread[first : first + 3 * CH]
            slab[dx, 0] = jnp.concatenate([taps, none], axis=0)
            slab[dx, 1] = jnp.concatenate([none, taps], axis=0)

        def columns(*which):
            out = blank
            for g, key in enumerate(which):
                if key is not None:
                    out = jnp.where(group == g, slab[key], out)
            return out.astype(bf16)

        rows = slice(dz * 4 * CH, (dz + 1) * 4 * CH)
        band[0, rows, : 4 * CH] = columns((1, 0), (1, 1), (0, 0), (0, 1))
        band[0, rows, 4 * CH :] = columns((2, 0), (2, 1), None, None)
        band[1, rows, : 4 * CH] = columns((0, 0), (0, 1), (1, 0), (1, 1))
        band[1, rows, 4 * CH :] = columns(None, None, (2, 0), (2, 1))


def combine(even, odd):
    rows = even.shape[0]
    low = iota((rows, 128), 1) < 64
    across = iota((rows, 128), 0) % WE
    centre = jnp.where(low, even[:, :128], odd[:, :128])
    before = pltpu.roll(jnp.where(low, odd[:, :128], even[:, :128]), 64, 1)
    after = jnp.where(low, even[:, 128:], odd[:, 128:])
    return (
        centre
        + jnp.where(across == 0, 0.0, pltpu.roll(before, 1, 0))
        + jnp.where(across == WE - 1, 0.0, pltpu.roll(after, rows - 1, 0))
    )


def view_first(padded, w, b, step):
    out = []
    for dz in range(3):
        rows = slice(dz * WE, dz * WE + ROWS)
        if b < 7:
            out.append(padded[w, rows, b * step : (b + 2) * step])
        else:
            out.append(padded[w, rows, 7 * step :])
            out.append(padded[w, rows, :step])
    return jnp.concatenate(out, axis=1)


def conv_first(padded, w, band, hidden, quarters):
    step = padded.shape[2] // 8
    for q in quarters:
        res = [
            lax.dot_general(
                view_first(padded, w, 2 * q + odd, step),
                band[kind],
                (((1,), (1,)), ((), ())),
                preferred_element_type=f32,
            )
            for odd, kind in ((0, 0), (1, 2 if q == 3 else 1))
        ]
        hidden[:, q * 128 : (q + 1) * 128] = combine(*res)


def conv_second(evens, odds, w, band, hidden, quarters):
    for q in quarters:
        res = [
            jnp.dot(
                jnp.concatenate(
                    [src[w, dz * WE : dz * WE + ROWS, q * 128 : (q + 1) * 128] for dz in range(3)], axis=1
                ),
                band[kind],
                preferred_element_type=f32,
            )
            for kind, src in enumerate((evens, odds))
        ]
        hidden[:, q * 128 : (q + 1) * 128] = combine(*res)


def over_voxels(row):
    row = row + pltpu.roll(row, 64, 1)
    return row + pltpu.roll(row, 32, 1)


def partial_sum(block):
    return jnp.sum(block.reshape(ROWS // 8, 8, 128), axis=0)


def statistics(hidden, gain):
    voxels = float(WE * WE * WE)
    about = over_voxels(hidden[:1, :128]) / 4.0
    first, square = None, None
    for q in range(4):
        off = hidden[:, q * 128 : (q + 1) * 128] - about
        parts = partial_sum(off), partial_sum(off * off)
        first = parts[0] if first is None else first + parts[0]
        square = parts[1] if square is None else square + parts[1]
    first = over_voxels(jnp.sum(first, axis=0, keepdims=True)) / voxels
    square = over_voxels(jnp.sum(square, axis=0, keepdims=True)) / voxels
    variance = jnp.maximum(square - first * first, 0.0)
    return about + first, lax.rsqrt(variance + epsilon) * gain


def normalize(hidden, stats, shift):
    mean_value, factor = stats
    out = []
    for q in range(4):
        scaled = (hidden[:, q * 128 : (q + 1) * 128] - mean_value) * factor + shift
        out.append(jnp.maximum(scaled, leak_slope * scaled))
    return out


def store_normed(values, evens, odds, w):
    rows = slice(WE, WE + ROWS)
    lane = iota((ROWS, 128), 1)
    for q in range(4):
        even = values[q] if q < 3 else jnp.where(lane >= 96, 0.0, values[q])
        evens[w, rows, q * 128 : (q + 1) * 128] = even.astype(bf16)
        here, after = values[q].astype(bf16), values[(q + 1) % 4].astype(bf16)
        odd = jnp.concatenate([here[:, 64:], after[:, :64]], axis=1)
        odds[w, rows, q * 128 : (q + 1) * 128] = odd if q < 3 else jnp.where(lane < 32, jnp.zeros((), bf16), odd)


def bell(at):
    off = at.astype(f32) - (WE - 1) / 2.0
    return -(off * off) / (2.0 * (WE / 4.0) ** 2)


def prepare_head(corner, live, head_weight, placed, head, gauss):
    cz, cx, cy = corner
    row = iota((ROWS, 128), 0)
    lane = iota((ROWS, 128), 1)
    source = ((row - cz) & (WE - 1)) * WE + ((lax.shift_right_logical(row, 4) - cx) & (WE - 1))
    for half in range(2):
        lanes = slice(half * 128, (half + 1) * 128)
        placed[:, lanes] = one_hot(source == lane + half * 128).astype(bf16)
        z, x = lax.shift_right_logical(row, 4), row & (WE - 1)
        y = (lax.shift_right_logical(lane, 4) + half * 8 - cy) & (WE - 1)
        gauss[:, lanes] = jnp.where(live, jnp.exp(bell(z) + bell(x) + bell(y)), 0.0)
    at = lax.shift_right_logical(iota((CH, WCLS), 1), 4) - cy
    for u in range(WE):
        head[u * CH : (u + 1) * CH, :] = jnp.where(((at - u - 2) & (WE - 1)) == 0, head_weight, 0.0).astype(bf16)


def apply_head(values, placed, head, gauss, bias):
    second = jnp.concatenate([v.astype(bf16) for v in values], axis=1)
    logits = jnp.dot(second, head[...], preferred_element_type=f32) + bias
    weighted = (logits * gauss[...]).astype(bf16)
    return jnp.dot(placed[...], weighted, preferred_element_type=f32).astype(bf16)


def places_of(span, sub):
    edge = min(span, WE - span)
    begin = jnp.where(sub == 0, WE - edge, 0)
    base = (1 - sub) * (WE - span)
    positions = [edge + m for m in range(span - edge)] + [begin + e for e in range(edge)]
    return [(p, p - base) for p in positions]


def masks_of(meta, sources, tile):
    lane_y = lax.shift_right_logical(iota((TZ, LANES), 1), 4)
    depth = iota((TZ, LANES), 0)
    masks = {}
    for k, w in sources:
        cz, cx, cy = (
            jnp.concatenate([meta[k, 3 * w + c : 3 * w + c + 1, :].astype(jnp.int32)] * (LANES // 128), axis=1)
            for c in range(3)
        )
        inside = (lane_y >= cy) & (lane_y < cy + WE)
        deep = (depth >= cz) if k < 2 else ((depth < cz) & (tile > 0))
        masks[k, w] = inside & deep, cx[:, :WCLS]
    return masks


def masked(part, mask, x):
    zy, cx = mask
    part = jnp.where((cx <= x) & (x < cx + WE), part, 0.0)
    wide = jnp.concatenate([part] * -(-LANES // WCLS), axis=1)[:, :LANES]
    return jnp.where(zy, wide, 0.0)


def cut(kind, piece, first_id, count):
    first, size = piece
    out, at = [], 0
    for c in range(count):
        rows = -(-(size - at) // (count - c))
        if rows:
            out.append((kind, first + at, rows, first_id + c))
            at += rows
    return out


def decode_send_kernel(
    features, taps_first, gain_first, shift_first, taps_second, gain_second, shift_second,
    head_weight, head_bias, corners_in, counts_in,
    tail, tail_sib, meta, acc,
    own, sib, padded, evens, odds, band_first, band_second, hidden, ready, got, placed, head, gauss,
    taps_one, taps_two, gains, weights, biases, corners, counts,
    load_sems, in_sems, x_send, x_recv, s_send, s_recv, z_send, z_recv, f_send, f_recv, m_send, m_recv,
):
    n = padded.shape[0]
    fold, sub, tile = (lax.axis_index(a) for a in ("folds", "sub", "tiles"))
    folds, subs, tiles = (lax.axis_size(a) for a in ("folds", "sub", "tiles"))
    span = VX // (folds * subs)
    edge = min(span, WE - span)
    loads = [
        pltpu.make_async_copy(features.at[w], padded.at[w, WE : WE + ROWS, :], load_sems.at[w])
        for w in range(n)
    ]
    small = [
        pltpu.make_async_copy(src, dst, in_sems.at[k])
        for k, (src, dst) in enumerate(
            (
                (corners_in, corners),
                (counts_in, counts),
                (head_weight, weights),
                (taps_first, taps_one),
                (taps_second, taps_two),
                (head_bias, biases),
                (gain_first, gains.at[0]),
                (shift_first, gains.at[1]),
                (gain_second, gains.at[2]),
                (shift_second, gains.at[3]),
            )
        )
    ]
    loads[0].start()
    for copy in small:
        copy.start()
    for load in loads[1:]:
        load.start()

    barrier = pltpu.get_barrier_semaphore()
    other = 1 - sub
    later, earlier = lax.rem(tile + 1, tiles), lax.rem(tile + tiles - 1, tiles)

    def greet(**where):
        pl.semaphore_signal(barrier, inc=1, device_id=where, device_id_type=MESH)

    def greet_tile(at):
        greet(tiles=at)
        greet(tiles=at, sub=other)
        for d in range(1, folds):
            greet(tiles=at, folds=lax.rem(fold + d, folds))

    greet(sub=other)
    for d in range(1, folds):
        greet(folds=lax.rem(fold + d, folds))

    @pl.when(tile < tiles - 1)
    def _():
        greet_tile(tile + 1)

    @pl.when(tile > 0)
    def _():
        greet_tile(tile - 1)

    for w in range(n):
        for ref in (padded, evens, odds):
            ref[w, :WE, :] = jnp.zeros((WE, ref.shape[2]), bf16)
            ref[w, WE + ROWS :, :] = jnp.zeros((WE, ref.shape[2]), bf16)
    for copy in small[:3]:
        copy.wait()
    pick = one_hot(iota((CLASSES, WCLS), 0) == iota((CLASSES, WCLS), 1) % CLASSES)
    head_rows = lax.dot_general(
        weights[...], pick.astype(bf16), (((0,), (0,)), ((), ())), preferred_element_type=f32
    )
    live_count = counts[sub, tile]
    for w in range(n):
        corner = corners[w, 0], corners[w, 1], corners[w, 2]
        prepare_head(corner, w < live_count, head_rows, placed.at[w], head.at[w], gauss.at[w])
    row_id = iota((8, 128), 0)
    corner_rows = jnp.zeros((8, 128), f32)
    for w in range(n):
        for c in range(3):
            at = corners[w, c].astype(f32)
            at = at - (tile * TZ).astype(f32) if c == 0 else at
            corner_rows = jnp.where(row_id == 3 * w + c, at, corner_rows)
    meta[0] = corner_rows
    for copy in small[3:]:
        copy.wait()
    build_first(taps_one, band_first)
    build_second(taps_two, band_second)
    gain_one, shift_one, gain_two, shift_two = (spread_lanes(gains[k], 128) for k in range(4))
    bias = spread_lanes(biases[...], WCLS)

    theirs = (jnp.where(sub == 0, 0, WE - edge), edge)
    shared = (edge, WE - 2 * edge)
    mine = (jnp.where(sub == 0, WE - edge, 0), edge)
    shared_piece = [("shared", *shared, 0)] if 2 * span > WE else []
    whole = shared_piece + [("theirs", *theirs, 1), ("mine", *mine, 2)]
    order = [whole] * (n - 1) + [shared_piece + cut("theirs", theirs, 1, 2) + cut("mine", mine, 4, 3)]

    def start_of(f):
        return lax.rem(f * (subs * span) + span, WE)

    def remote(src, dst, sems, at, **where):
        return pltpu.make_async_remote_copy(
            src_ref=src, dst_ref=dst, send_sem=sems[0].at[at], recv_sem=sems[1].at[at],
            device_id=where, device_id_type=MESH,
        )

    x_copies, s_copies, z_copies, f_copies = {}, {}, {}, {}
    metas = [
        remote(meta.at[0], meta.at[1], (m_send, m_recv), 0, sub=other),
        remote(meta.at[0], meta.at[2], (m_send, m_recv), 1, tiles=later),
        remote(meta.at[0], meta.at[3], (m_send, m_recv), 2, tiles=later, sub=other),
    ]

    def norm_one(w):
        stats[w, 1] = statistics(hidden.at[w], gain_one)

    def store_one(w):
        store_normed(normalize(hidden.at[w], stats[w, 1], shift_one), evens, odds, w)

    def norm_two(w):
        stats[w, 2] = statistics(hidden.at[w], gain_two)

    def values_two(w):
        values[w] = normalize(hidden.at[w], stats[w, 2], shift_two)

    def finish(w):
        out = apply_head(values[w], placed.at[w], head.at[w], gauss.at[w], bias).reshape(WE, WE, WCLS)
        ready[w, :WE] = out
        ready[w, WE:] = out

    stats, values = {}, {}

    def send(w):
        if w == 0:
            neighbours = (tile + tiles - 1) // tiles + (2 * tiles - 2 - tile) // tiles
            pl.semaphore_wait(barrier, folds + neighbours * (folds + 1))

        for _, first, size, at in order[w]:
            for d in range(1, folds):
                peer = lax.rem(fold + d, folds)
                copy = remote(
                    ready.at[w, pl.ds(start_of(peer) + first, size)],
                    got.at[d - 1, w, pl.ds(first, size)],
                    (x_send, x_recv), (d - 1, w, at), folds=peer,
                )
                copy.start()
                x_copies[d, w, at] = copy
        if w == 0:
            metas[0].start()

            @pl.when(tile < tiles - 1)
            def _():
                for copy in metas[1:]:
                    copy.start()

    def first(w, *quarters):
        conv_first(padded, w, band_first, hidden.at[w], quarters)

    def second(w, *quarters):
        conv_second(evens, odds, w, band_second, hidden.at[w], quarters)

    loads[0].wait()
    loads[1].wait()
    first(0, 0, 1, 2, 3)
    norm_one(0)
    store_one(0)
    second(0, 0, 1, 2, 3)
    norm_two(0)
    values_two(0)
    finish(0)
    send(0)
    first(1, 0, 1, 2, 3)
    norm_one(1)
    store_one(1)
    second(1, 0, 1, 2, 3)
    norm_two(1)
    values_two(1)
    finish(1)
    send(1)

    def gather(w, kind, first, size, at):
        rows = pl.ds(first, size)
        total = ready[w, pl.ds(start_of(fold) + first, size)].astype(f32)
        for d in range(1, folds):
            x_copies[d, w, at].wait_recv()
            total = total + got[d - 1, w, rows].astype(f32)
        own[w, rows] = total.astype(bf16)
        key = w, at
        if kind == "theirs":
            z_copies[key] = remote(
                own.at[w, rows], tail_sib.at[w, rows], (z_send, z_recv), key, tiles=later, sub=other
            )
        elif True:
            z_copies[key] = remote(own.at[w, rows], tail.at[w, rows], (z_send, z_recv), key, tiles=later)
        if key in z_copies:

            @pl.when(tile < tiles - 1)
            def _():
                z_copies[key].start()

        if kind != "mine":
            s_copies[key] = remote(own.at[w, rows], sib.at[w, rows], (s_send, s_recv), key, sub=other)
            s_copies[key].start()

    def forward(w):
        if shared_piece:
            rows = pl.ds(*shared)
            f_copies[w] = remote(tail.at[w, rows], tail_sib.at[w, rows], (f_send, f_recv), w, sub=other)

            @pl.when(tile > 0)
            def _():
                z_copies[w, 0].wait_recv()
                f_copies[w].start()

    for w in range(n - 1):
        for piece in order[w]:
            gather(w, *piece)
    last = n - 1
    early = [p for p in order[last] if p[0] != "mine"]
    for piece in early:
        gather(last, *piece)
    for w in range(n - 1):
        forward(w)
    x0 = (fold * subs + sub) * span
    refs = own, sib, tail, tail_sib

    def accumulate(sources, fresh):
        masks = masks_of(meta, sources, tile)
        for r, (position, i) in enumerate(places_of(span, sub)):
            total = None if fresh else acc[r]
            for k, w in sources:
                part = masked(refs[k][w, position].astype(f32), masks[k, w], x0 + i)
                total = part if total is None else total + part
            acc[r] = total

    metas[0].wait()
    for (w, _), copy in s_copies.items():
        if w < last:
            copy.wait()

    accumulate([(k, w) for k in range(2) for w in range(last)], True)
    for piece in order[last][len(early) :]:
        gather(last, *piece)

    @pl.when(tile > 0)
    def _():
        for copy in metas[1:]:
            copy.wait_recv()
        for (w, at), copy in z_copies.items():
            if w < last and not (at == 0 and w in f_copies):
                copy.wait_recv()
        for copy in f_copies.values():
            copy.wait()

    for (w, _), copy in s_copies.items():
        if w == last:
            copy.wait()
    accumulate([(k, w) for k in (2, 3) for w in range(last)] + [(0, last), (1, last)], False)

    forward(last)

    @pl.when(tile > 0)
    def _():
        for (w, at), copy in z_copies.items():
            if w == last and not (at == 0 and w in f_copies):
                copy.wait_recv()
        if last in f_copies:
            f_copies[last].wait()

    for copy in x_copies.values():
        copy.wait_send()

    @pl.when(tile < tiles - 1)
    def _():
        for copy in metas[1:] + list(z_copies.values()):
            copy.wait_send()


def decode_send(features, taps_first, gf, sf, taps_second, gs, ss, hw, hb, corners, counts):
    n = features.shape[0]
    in_width = features.shape[-1]
    cin = in_width // WE
    folds, subs, tiles = (lax.axis_size(a) for a in ("folds", "sub", "tiles"))
    span = VX // (folds * subs)
    edge = min(span, WE - span)
    hbm = pl.BlockSpec(memory_space=pltpu.HBM)
    vmem = pl.BlockSpec(memory_space=pltpu.VMEM)
    dma = pltpu.SemaphoreType.DMA
    block = pltpu.VMEM((n, WE, WE, WCLS), bf16)
    return pl.pallas_call(
        decode_send_kernel,
        out_shape=[block, block, pltpu.VMEM((4, 8, 128), f32), pltpu.VMEM((span, TZ, LANES), f32)],
        in_specs=[hbm] * 11,
        out_specs=[vmem] * 4,
        scratch_shapes=[
            pltpu.VMEM((n, WE, WE, WCLS), bf16),
            pltpu.VMEM((n, WE, WE, WCLS), bf16),
            pltpu.VMEM((n, ROWS + 2 * WE, in_width), bf16),
            pltpu.VMEM((n, ROWS + 2 * WE, WIDTH), bf16),
            pltpu.VMEM((n, ROWS + 2 * WE, WIDTH), bf16),
            pltpu.VMEM((3, 8 * CH, 12 * cin), bf16),
            pltpu.VMEM((2, 12 * CH, 8 * CH), bf16),
            pltpu.VMEM((n, ROWS, WIDTH), f32),
            pltpu.VMEM((n, 2 * WE, WE, WCLS), bf16),
            pltpu.VMEM((folds - 1, n, WE, WE, WCLS), bf16),
            pltpu.VMEM((n, ROWS, ROWS), bf16),
            pltpu.VMEM((n, WIDTH, WCLS), bf16),
            pltpu.VMEM((n, ROWS, WCLS), f32),
            pltpu.VMEM((27 * CH, cin), bf16),
            pltpu.VMEM((27 * CH, CH), bf16),
            pltpu.VMEM((4, 1, CH), f32),
            pltpu.VMEM((CLASSES, CH), bf16),
            pltpu.VMEM((1, CLASSES), f32),
            pltpu.SMEM((n, 3), jnp.int32),
            pltpu.SMEM((subs, tiles), jnp.int32),
            dma((n,)),
            dma((10,)),
            dma((folds - 1, n, 8)),
            dma((folds - 1, n, 8)),
            dma((n, 8)),
            dma((n, 8)),
            dma((n, 8)),
            dma((n, 8)),
            dma((n,)),
            dma((n,)),
            dma((3,)),
            dma((3,)),
        ],
        compiler_params=pltpu.CompilerParams(
            collective_id=0, has_side_effects=True, vmem_limit_bytes=56 * 1024 * 1024
        ),
    )(
        features.reshape(n, ROWS, in_width),
        taps_first.swapaxes(-1, -2).reshape(27 * CH, cin),
        gf,
        sf,
        taps_second.reshape(27 * CH, CH),
        gs,
        ss,
        hw.T,
        hb,
        corners,
        counts.T,
    )


def place_kernel(tail, tail_sib, meta, acc, out, rows, sems):
    n = tail_sib.shape[0]
    fold, sub, tile = (lax.axis_index(a) for a in ("folds", "sub", "tiles"))
    folds, subs = lax.axis_size("folds"), lax.axis_size("sub")
    span = out.shape[0]
    x0 = (fold * subs + sub) * span
    w = n - 1
    masks = masks_of(meta, ((2, w), (3, w)), tile)
    copies = []
    for r, (position, i) in enumerate(places_of(span, sub)):
        part = tail[w, position].astype(f32)
        total = acc[r] + masked(part, masks[2, w], x0 + i)
        part = tail_sib[w, position].astype(f32)
        rows[r] = total + masked(part, masks[3, w], x0 + i)
        copy = pltpu.make_async_copy(rows.at[r], out.at[i], sems.at[r])
        copy.start()
        copies.append(copy)
    for copy in copies:
        copy.wait()


def place(*blocks):
    span = VX // (lax.axis_size("folds") * lax.axis_size("sub"))
    vmem = pl.BlockSpec(memory_space=pltpu.VMEM)
    return pl.pallas_call(
        place_kernel,
        out_shape=jax.ShapeDtypeStruct((span, TZ, LANES), f32),
        in_specs=[vmem] * 4,
        out_specs=pl.BlockSpec(memory_space=pltpu.HBM),
        scratch_shapes=[pltpu.VMEM((span, TZ, LANES), f32), pltpu.SemaphoreType.DMA((span,))],
        compiler_params=pltpu.CompilerParams(vmem_limit_bytes=12 * 1024 * 1024),
    )(*blocks)


def on_device(features, conv_one, gain_one, shift_one, conv_two, gain_two, shift_two, head_weight, head_bias, corners, counts):
    blocks = decode_send(
        features[0], conv_one[0], gain_one, shift_one, conv_two[0], gain_two, shift_two,
        head_weight[0], head_bias, corners, counts,
    )
    return place(*blocks).transpose(1, 0, 2)


def solution(mesh):
    windows = ("groups", "tiles", "sub")
    placed = (
        P("folds", windows, None, None, None),
        P("folds", None, None, None, None, None),
        P("folds", None),
        P("folds", None),
        P("folds", None, None, None, None, None),
        P("folds", None),
        P("folds", None),
        P("folds", None, None),
        P("folds", None),
        P(windows, None),
        P("groups", None),
    )
    return jax.shard_map(
        on_device,
        mesh=mesh,
        in_specs=placed,
        out_specs=P(("groups", "tiles"), ("folds", "sub"), None),
        check_vma=False,
    )
```
